256 devices in a mesh: dp: 64 (over y, z, core), mp: 4 (over x).
Axes of the slice: x: 4, y: 4, z: 8, core: 2. Of those that a mesh axis runs over, the one named last changes fastest.
Arguments:
- features: bfloat16 [262144, 1024], P('dp', 'mp'), may hold values from -6 to 6
- history: bfloat16 [131072, 1024], P('dp', 'mp'), may hold values from -6 to 6
- adj_values: bfloat16 [2048, 8, 128, 128], P('dp'), may hold values from -0.1875 to 0.1875
- adj_sources: int32 [2048, 8], P('dp'), may hold values from 0 to 191, as said below
- pull_list: int32 [64, 64, 2], P('dp'), may hold values from 0 to 15
- pull_count: int32 [64, 64], P('dp'), may hold values from 0 to 2, as said below
- partner_mask: int32 [1], replicated, may hold values from 1 to 63
- weight: bfloat16 [1024, 1024], P('mp'), may hold values from -0.1875 to 0.1875
- bias: float32 [1024], P('mp'), may hold values from -3 to 3
Outputs:
- layer_out: bfloat16 [262144, 1024], P('dp', 'mp')
The draws below stay inside these ranges and needn't reach their ends.
Inputs may be any that keep to these rules, and one draw needn't show every extreme that they name: The partner of cluster c is cluster c XOR partner_mask[0]. Slots s >= pull_count[c, o] of pull_list[c, o] are not live; in every draw some owner has all 2 slots live for every cluster. `adj_sources`: indexes sources: own blocks, then partner blocks, then pulled slots; tile 0 of every target block names an own block and tile 1 a partner block. `pull_list`: local block numbers within an owner's history.
All inputs are finite; a program needn't handle non-finite values.
Results may differ from the reference program's by a relative error of at most 0.0045.
Values may be sent and summed in bfloat16 or wider, within the bound.
A program may use at most 128 MiB of HBM per device.

```python
import jax
import jax.numpy as jnp
from jax import lax

D = 1024
RB = 32
KB = 8
CAP = 2
HBLK = 16
NODES = 262144
HNODES = 131072
NSRC = 192
N_DP = 64


def draw_pull_count(key, part):
    base_counts = jax.random.randint(key, (N_DP, N_DP), 0, CAP + 1)
    hot_owner = jax.random.randint(jax.random.fold_in(key, 7), (), 0, N_DP)
    column_ids = jnp.arange(N_DP, dtype=jnp.int32)
    filled = jnp.where((column_ids == hot_owner)[None, :], CAP, base_counts)
    return filled.astype(jnp.int32)


def draw_adj_sources(key, part):
    total_rows = N_DP * RB
    spread_src = jax.random.randint(jax.random.fold_in(key, 11), (total_rows, KB), 0, NSRC)
    own_src = jax.random.randint(jax.random.fold_in(key, 12), (total_rows, KB), 0, RB)
    partner_src = RB + jax.random.randint(jax.random.fold_in(key, 13), (total_rows, KB), 0, RB)
    tile_ids = jnp.arange(KB, dtype=jnp.int32)[None, :]
    row_ids = jnp.arange(total_rows, dtype=jnp.int32)[:, None]
    chosen = jnp.where(tile_ids == 0, own_src, jnp.where(tile_ids == 1, partner_src, spread_src))
    chosen = jnp.where((row_ids == 0) & (tile_ids == KB - 1), NSRC - 1, chosen)
    return chosen.astype(jnp.int32)


def plant(entries, own_key, smallest, top_value):
    longest = entries.shape.index(max(entries.shape))
    spots = []
    for shift in (0, 1):
        where = [jax.random.randint(jax.random.fold_in(own_key, axis), (), 0, length) for axis, length in enumerate(entries.shape)]
        where[longest] = (where[longest] + shift) % entries.shape[longest]
        spots.append(tuple(where))
    return entries.at[spots[0]].set(smallest).at[spots[1]].set(top_value)


def block_levels(own_key, extent, pieces, smallest, top_value):
    def one(axis_at, blocks):
        draws = jax.random.uniform(jax.random.fold_in(jax.random.fold_in(own_key, 6), axis_at), (blocks,), jnp.float32, smallest / len(pieces), top_value / len(pieces))
        return jnp.repeat(jnp.exp(draws), extent[axis_at] // blocks).reshape((-1,) + (1,) * (len(extent) - axis_at - 1))

    loudness = one(*pieces[0])
    for cut in pieces[1:]:
        loudness = loudness * one(*cut)
    return loudness


def noise(rng, extent, width, limit, split=(), held_as=jnp.bfloat16):
    level = block_levels(rng, extent, split, -0.22, 0.18) if split else 1.0
    values = jax.random.normal(rng, extent, jnp.float32) * width * level
    return jnp.minimum(jnp.maximum(values, -limit), limit).astype(held_as)


def setup_inputs(seed: int = 0) -> dict:
    keys = jax.random.split(jax.random.key(seed), 10)
    return {
        "features": noise(keys[0], (NODES, D), 1.0, 6.0, ((0, 64), (1, 4))),
        "history": noise(keys[1], (HNODES, D), 1.0, 6.0, ((0, 64), (1, 4))),
        "adj_values": noise(keys[2], (N_DP * RB, KB, 128, 128), (KB * 128) ** -0.5, 0.1875, ((0, 64),)),
        "adj_sources": draw_adj_sources(jax.random.fold_in(keys[9], 71), 0),
        "pull_list": plant(jax.random.randint(keys[4], (N_DP, N_DP, CAP), 0, HBLK), jax.random.fold_in(keys[4], 1), 0, HBLK - 1).astype(jnp.int32),
        "pull_count": draw_pull_count(jax.random.fold_in(keys[9], 71), 0),
        "partner_mask": jax.random.randint(keys[6], (1,), 1, N_DP).astype(jnp.int32),
        "weight": noise(keys[7], (D, D), D ** -0.5, 0.1875, ((0, 4),)),
        "bias": noise(keys[8], (D,), 0.5, 3.0, ((0, 4),), jnp.float32),
    }


def reference(features, history, adj_values, adj_sources, pull_list, pull_count, partner_mask, weight, bias):
    row_count = RB * 128
    hist_blocks = history.reshape(N_DP * HBLK, 128, D)
    owner_ids = jnp.arange(N_DP, dtype=jnp.int32)
    slot_ids = jnp.arange(CAP, dtype=jnp.int32)

    def one_cluster(cluster):
        own_rows = lax.dynamic_slice_in_dim(features, cluster * row_count, row_count, 0)
        partner = jnp.bitwise_xor(cluster, partner_mask[0]).astype(jnp.int32)
        partner_rows = lax.dynamic_slice_in_dim(features, partner * row_count, row_count, 0)
        wanted = owner_ids[:, None] * HBLK + pull_list[cluster]
        pulled = hist_blocks[wanted]
        live_slots = slot_ids[None, :] < pull_count[cluster][:, None]
        pulled = jnp.where(live_slots[:, :, None, None], pulled, jnp.zeros((), pulled.dtype))
        sources = jnp.concatenate([own_rows.reshape(RB, 128, D), partner_rows.reshape(RB, 128, D),
                                   pulled.reshape(N_DP * CAP, 128, D)], axis=0)
        tile_values = lax.dynamic_slice_in_dim(adj_values, cluster * RB, RB, 0)
        picked_src = lax.dynamic_slice_in_dim(adj_sources, cluster * RB, RB, 0)
        gathered = sources[picked_src].astype(jnp.float32)
        agg = jnp.einsum('tkij,tkjd->tid', tile_values.astype(jnp.float32), gathered)
        agg = agg.reshape(row_count, D).astype(jnp.bfloat16)
        mixed = jnp.dot(agg, weight, preferred_element_type=jnp.float32) + bias
        return jnp.maximum(mixed, 0.0).astype(jnp.bfloat16)

    results = lax.map(one_cluster, jnp.arange(N_DP, dtype=jnp.int32))
    return results.reshape(N_DP * row_count, D)
```

```python
import functools

import jax
import jax.numpy as jnp
from jax import lax
from jax.experimental import pallas as pl
from jax.experimental.pallas import tpu as pltpu
from jax.sharding import Mesh, PartitionSpec as P

NY, NZ, NC = 4, 8, 2
BLK = 128


def aggregate_kernel(src_idx, live, own, partner, pulled, adj, out, srcs, sems):
    t = pl.program_id(0)
    nb = own.shape[0]

    @pl.when(t == 0)
    def _():
        copies = [
            pltpu.make_async_copy(own, srcs.at[pl.ds(0, nb)], sems.at[0]),
            pltpu.make_async_copy(partner, srcs.at[pl.ds(nb, nb)], sems.at[1]),
            pltpu.make_async_copy(pulled, srcs.at[pl.ds(2 * nb, pulled.shape[0])], sems.at[2]),
        ]
        for copy in copies:
            copy.start()
        for copy in copies:
            copy.wait()

    kb = adj.shape[1]
    tiles, blocks = [], []
    for k in range(kb):
        tile = adj[0, k]
        tiles.append(jnp.where(live[t * kb + k] > 0, tile, jnp.zeros_like(tile)))
        blocks.append(srcs[src_idx[t * kb + k]])
    lhs = jnp.concatenate(tiles, axis=1)
    rhs = jnp.concatenate(blocks, axis=0)
    out[...] = jnp.dot(lhs, rhs, preferred_element_type=jnp.float32).astype(out.dtype)


def aggregate(src_idx, live, own, partner, pulled, adj):
    tb, kb = adj.shape[:2]
    width = own.shape[-1]
    n_src = own.shape[0] + partner.shape[0] + pulled.shape[0]
    return pl.pallas_call(
        aggregate_kernel,
        out_shape=jax.ShapeDtypeStruct((tb * BLK, width), jnp.bfloat16),
        grid_spec=pltpu.PrefetchScalarGridSpec(
            num_scalar_prefetch=2,
            grid=(tb,),
            in_specs=[
                pl.BlockSpec(memory_space=pl.ANY),
                pl.BlockSpec(memory_space=pl.ANY),
                pl.BlockSpec(memory_space=pl.ANY),
                pl.BlockSpec((1, kb, BLK, BLK), lambda t, *_: (t, 0, 0, 0)),
            ],
            out_specs=pl.BlockSpec((BLK, width), lambda t, *_: (t, 0)),
            scratch_shapes=[
                pltpu.VMEM((n_src, BLK, width), jnp.bfloat16),
                pltpu.SemaphoreType.DMA((3,)),
            ],
        ),
        compiler_params=pltpu.CompilerParams(vmem_limit_bytes=32 << 20),
        name="aggregate",
    )(src_idx, live, own, partner, pulled, adj)


def xor_permute(value, axes, size, which):
    def branch(m):
        if m == 0:
            return lambda v: v
        pairs = [(s, s ^ m) for s in range(size)]
        return lambda v: lax.ppermute(v, axes, pairs)

    return lax.switch(which, [branch(m) for m in range(size)], value)


def per_device(
    features, history, adj_values, adj_sources, pull_list, pull_count, partner_mask, weight, bias
):
    row_count, width = features.shape
    row_blocks = row_count // BLK
    cap = pull_list.shape[-1]
    hist_blocks = history.shape[0] // BLK
    mask = partner_mask[0]
    yc_mask = (mask >> 4) * NC + (mask & 1)
    z_mask = (mask >> 1) & (NZ - 1)

    hist_z = lax.all_gather(history, "z", axis=0, tiled=True)
    wanted = pull_list[0].reshape(NY, NZ, NC, cap).transpose(0, 2, 1, 3).reshape(NY * NC, NZ, cap)
    asked = lax.all_to_all(wanted, ("y", "core"), split_axis=0, concat_axis=0, tiled=True)
    block_ids = asked + jnp.arange(NZ, dtype=jnp.int32)[None, :, None] * hist_blocks

    half_way = xor_permute(features, ("y", "core"), NY * NC, yc_mask)
    hist_z, half_way, block_ids = lax.optimization_barrier((hist_z, half_way, block_ids))

    picked = hist_z.reshape(NZ * hist_blocks, BLK, width)[block_ids]
    pulled = lax.all_to_all(picked, ("y", "core"), split_axis=0, concat_axis=0, tiled=True)
    partner_rows = xor_permute(half_way, "z", NZ, z_mask)

    slot_no = jnp.maximum(adj_sources - 2 * row_blocks, 0)
    owner, slot = slot_no // cap, slot_no % cap
    oy, oz, oc = owner // (NZ * NC), (owner // NC) % NZ, owner % NC
    moved = ((oy * NC + oc) * NZ + oz) * cap + slot
    is_pulled = adj_sources >= 2 * row_blocks
    src_idx = jnp.where(is_pulled, 2 * row_blocks + moved, adj_sources)
    alive = (jnp.arange(cap)[None, :] < pull_count[0][:, None]).reshape(-1)
    live = jnp.where(is_pulled, alive[slot_no], True).astype(jnp.int32)

    agg = aggregate(
        src_idx.reshape(-1),
        live.reshape(-1),
        features.reshape(row_blocks, BLK, width),
        partner_rows.reshape(row_blocks, BLK, width),
        pulled.reshape(-1, BLK, width),
        adj_values,
    )
    w_cols = lax.all_to_all(weight, "mp", split_axis=1, concat_axis=0, tiled=True)
    agg_all = lax.all_gather(agg, "mp", axis=1, tiled=True)
    mixed = jnp.dot(agg_all, w_cols, preferred_element_type=jnp.float32)
    return jnp.maximum(mixed + bias, 0.0).astype(jnp.bfloat16)


def solution(mesh):
    n_mp = mesh.devices.shape[1]
    fine = Mesh(mesh.devices.reshape(NY, NZ, NC, n_mp), ("y", "z", "core", "mp"))
    dp = ("y", "z", "core")
    in_specs = (
        P(dp, "mp"),
        P(dp, "mp"),
        P(dp, None, None, None),
        P(dp, None),
        P(dp, None, None),
        P(dp, None),
        P(),
        P("mp", None),
        P("mp"),
    )
    return jax.shard_map(
        per_device, mesh=fine, in_specs=in_specs, out_specs=P(dp, "mp"), check_vma=False
    )
```

```python
import jax
import jax.numpy as jnp
from jax import lax
from jax.experimental import pallas as pl
from jax.experimental.pallas import tpu as pltpu
from jax.sharding import Mesh, PartitionSpec as P

NY, NZ, NC = 4, 8, 2
BLK = 128
CHUNKS = 4
MESH = pl.DeviceIdType.MESH


def layer_kernel(
    n_mp, src_idx, own, partner, pulled, adj, wts, bias, out,
    srcs, tiles, agg_out, agg_in, res_out, load_sem, send_a, recv_a, send_b, recv_b,
):
    me = lax.axis_index("mp")
    tb, kb = adj.shape[:2]
    nb, n_pulled = own.shape[0], pulled.shape[0]
    n_src = 2 * nb + n_pulled
    per_dev = tb // n_mp
    per_chunk = per_dev // CHUNKS
    rows = per_chunk * BLK

    loads = [
        pltpu.make_async_copy(own, srcs.at[pl.ds(0, nb)], load_sem.at[0]),
        pltpu.make_async_copy(partner, srcs.at[pl.ds(nb, nb)], load_sem.at[1]),
        pltpu.make_async_copy(pulled, srcs.at[pl.ds(2 * nb, n_pulled)], load_sem.at[2]),
        pltpu.make_async_copy(adj, tiles, load_sem.at[3]),
    ]
    for load in loads:
        load.start()
    srcs[n_src] = jnp.zeros(srcs.shape[1:], srcs.dtype)

    barrier = pltpu.get_barrier_semaphore()
    for k in range(1, n_mp):
        pl.semaphore_signal(barrier, inc=1, device_id={"mp": (me + k) % n_mp}, device_id_type=MESH)
    pl.semaphore_wait(barrier, n_mp - 1)
    for load in loads:
        load.wait()

    def to_rows(q, k):
        return pltpu.make_async_remote_copy(
            src_ref=agg_out.at[q, k - 1],
            dst_ref=agg_in.at[q, k],
            send_sem=send_a.at[q, k - 1],
            recv_sem=recv_a.at[q, k - 1],
            device_id={"mp": (me + k) % n_mp},
            device_id_type=MESH,
        )

    def to_columns(q, k):
        return pltpu.make_async_remote_copy(
            src_ref=res_out.at[q, k - 1],
            dst_ref=out.at[pl.ds(pl.multiple_of((me * CHUNKS + q) * rows, rows), rows)],
            send_sem=send_b.at[q, k - 1],
            recv_sem=recv_b.at[q, k - 1],
            device_id={"mp": (me + k) % n_mp},
            device_id_type=MESH,
        )

    def aggregate(q, k, dst):
        first = ((me + k) % n_mp) * per_dev + q * per_chunk

        def one(i, carry):
            t = first + i
            lhs = jnp.concatenate([tiles[t, j] for j in range(kb)], axis=1)
            rhs = jnp.concatenate([srcs[src_idx[t * kb + j]] for j in range(kb)], axis=0)
            block = jnp.dot(lhs, rhs, preferred_element_type=jnp.float32)
            dst[pl.ds(pl.multiple_of(i * BLK, BLK), BLK), :] = block.astype(dst.dtype)
            return carry

        lax.fori_loop(0, per_chunk, one, 0)

    def multiply(q):
        for k in range(1, n_mp):
            to_rows(q, k).wait_recv()
        for n in list(range(1, n_mp)) + [0]:
            part = bias[(n_mp - n) % n_mp] + jnp.zeros((rows, 1), jnp.float32)
            for k in range(n_mp):
                part = part + jnp.dot(
                    agg_in[q, k], wts[k, (me + n) % n_mp], preferred_element_type=jnp.float32
                )
            part = jnp.maximum(part, 0.0).astype(out.dtype)
            if n:
                res_out[q, n - 1] = part
                to_columns(q, n).start()
            else:
                out[pl.ds(pl.multiple_of((me * CHUNKS + q) * rows, rows), rows), :] = part

    for q in range(CHUNKS + 1):
        if q < CHUNKS:
            for k in (2, 1, 3, 0):
                if k:
                    aggregate(q, k, agg_out.at[q, k - 1])
                    to_rows(q, k).start()
                else:
                    aggregate(q, k, agg_in.at[q, 0])
        if q:
            multiply(q - 1)
    for q in range(CHUNKS):
        for k in range(1, n_mp):
            to_rows(q, k).wait_send()
            to_columns(q, k).wait()


def layer(src_idx, own, partner, pulled, adj, wts, bias):
    n_mp = wts.shape[0]
    tb, kb = adj.shape[:2]
    width = own.shape[-1]
    n_src = own.shape[0] + partner.shape[0] + pulled.shape[0]
    rows = tb // n_mp // CHUNKS * BLK
    any_spec = pl.BlockSpec(memory_space=pl.ANY)
    vmem_spec = pl.BlockSpec(memory_space=pltpu.VMEM)

    def kernel(*refs):
        layer_kernel(n_mp, *refs)

    return pl.pallas_call(
        kernel,
        out_shape=jax.ShapeDtypeStruct((tb * BLK, width), jnp.bfloat16),
        in_specs=[pl.BlockSpec(memory_space=pltpu.SMEM)] + [any_spec] * 4 + [vmem_spec] * 2,
        out_specs=vmem_spec,
        scratch_shapes=[
            pltpu.VMEM((n_src + 1, BLK, width), jnp.bfloat16),
            pltpu.VMEM(adj.shape, jnp.bfloat16),
            pltpu.VMEM((CHUNKS, n_mp - 1, rows, width), jnp.bfloat16),
            pltpu.VMEM((CHUNKS, n_mp, rows, width), jnp.bfloat16),
            pltpu.VMEM((CHUNKS, n_mp - 1, rows, width), jnp.bfloat16),
            pltpu.SemaphoreType.DMA((4,)),
        ]
        + [pltpu.SemaphoreType.DMA((CHUNKS, n_mp - 1))] * 4,
        compiler_params=pltpu.CompilerParams(
            collective_id=0, has_side_effects=True, vmem_limit_bytes=44 << 20
        ),
        name="layer",
    )(src_idx, own, partner, pulled, adj, wts, bias)


def xor_permute(value, axes, size, which):
    def branch(m):
        if m == 0:
            return lambda v: v
        pairs = [(s, s ^ m) for s in range(size)]
        return lambda v: lax.ppermute(v, axes, pairs)

    return lax.switch(which, [branch(m) for m in range(size)], value)


def from_all(value, axis):
    n = lax.axis_size(axis)
    moved = [lax.ppermute(value, axis, [(s, (s + k) % n) for s in range(n)]) for k in range(1, n)]
    return jnp.stack([value] + moved)


def per_device(
    features, history, adj_values, adj_sources, pull_list, pull_count, partner_mask, weight, bias
):
    row_count, width = features.shape
    row_blocks = row_count // BLK
    cap = pull_list.shape[-1]
    hist_blocks = history.shape[0] // BLK
    mask = partner_mask[0]
    n_mp = lax.axis_size("mp")
    yc_mask = (mask >> 4) * NC + (mask & 1)
    z_mask = (mask >> 1) & (NZ - 1)

    hist_z = lax.all_gather(history, "z", axis=0, tiled=True)
    wanted = pull_list[0].reshape(NY, NZ, NC, cap).transpose(0, 2, 1, 3).reshape(NY * NC, NZ, cap)
    asked = lax.all_to_all(wanted, ("y", "core"), split_axis=0, concat_axis=0, tiled=True)
    block_ids = asked + jnp.arange(NZ, dtype=jnp.int32)[None, :, None] * hist_blocks

    wts = from_all(weight.reshape(width, n_mp, width).transpose(1, 0, 2), "mp")
    biases = from_all(bias.reshape(1, width), "mp")

    half_way = xor_permute(features, ("y", "core"), NY * NC, yc_mask)
    hist_z, half_way, block_ids, wts, biases = lax.optimization_barrier(
        (hist_z, half_way, block_ids, wts, biases)
    )

    picked = hist_z.reshape(NZ * hist_blocks, BLK, width)[block_ids]
    pulled = lax.all_to_all(picked, ("y", "core"), split_axis=0, concat_axis=0, tiled=True)
    partner_rows = xor_permute(half_way, "z", NZ, z_mask)

    slot_no = jnp.maximum(adj_sources - 2 * row_blocks, 0)
    owner, slot = slot_no // cap, slot_no % cap
    oy, oz, oc = owner // (NZ * NC), (owner // NC) % NZ, owner % NC
    moved = ((oy * NC + oc) * NZ + oz) * cap + slot
    alive = (jnp.arange(cap)[None, :] < pull_count[0][:, None]).reshape(-1)
    n_pulled = NY * NZ * NC * cap
    pulled_src = 2 * row_blocks + jnp.where(alive[slot_no], moved, n_pulled)
    src_idx = jnp.where(adj_sources >= 2 * row_blocks, pulled_src, adj_sources)

    return layer(
        src_idx.reshape(-1),
        features.reshape(row_blocks, BLK, width),
        partner_rows.reshape(row_blocks, BLK, width),
        pulled.reshape(-1, BLK, width),
        adj_values,
        wts,
        biases,
    )


def solution(mesh):
    n_mp = mesh.devices.shape[1]
    fine = Mesh(mesh.devices.reshape(NY, NZ, NC, n_mp), ("y", "z", "core", "mp"))
    dp = ("y", "z", "core")
    in_specs = (
        P(dp, "mp"),
        P(dp, "mp"),
        P(dp, None, None, None),
        P(dp, None),
        P(dp, None, None),
        P(dp, None),
        P(),
        P("mp", None),
        P("mp"),
    )
    return jax.shard_map(
        per_device, mesh=fine, in_specs=in_specs, out_specs=P(dp, "mp"), check_vma=False
    )
```

```python
import jax
import jax.numpy as jnp
from jax import lax
from jax.experimental import pallas as pl
from jax.experimental.pallas import tpu as pltpu
from jax.sharding import Mesh, PartitionSpec as P

NY, NZ, NC = 4, 8, 2
BLK = 128
CHUNKS = 4
MESH = pl.DeviceIdType.MESH


def layer_kernel(
    n_mp, src_idx, own, partner, pulled, adj, wts, bias, out,
    srcs, tiles, agg_out, agg_in, res_out, load_sem, send_a, recv_a, send_b, recv_b,
):
    me = lax.axis_index("mp")
    tb, kb = adj.shape[:2]
    nb, n_pulled = own.shape[0], pulled.shape[0]
    n_src = 2 * nb + n_pulled
    per_dev = tb // n_mp
    per_chunk = per_dev // CHUNKS
    rows = per_chunk * BLK

    loads = [
        pltpu.make_async_copy(own, srcs.at[pl.ds(0, nb)], load_sem.at[0]),
        pltpu.make_async_copy(partner, srcs.at[pl.ds(nb, nb)], load_sem.at[1]),
        pltpu.make_async_copy(pulled, srcs.at[pl.ds(2 * nb, n_pulled)], load_sem.at[2]),
        pltpu.make_async_copy(adj, tiles, load_sem.at[3]),
    ]
    for load in loads:
        load.start()
    srcs[n_src] = jnp.zeros(srcs.shape[1:], srcs.dtype)

    barrier = pltpu.get_barrier_semaphore()
    for k in range(1, n_mp):
        pl.semaphore_signal(barrier, inc=1, device_id={"mp": (me + k) % n_mp}, device_id_type=MESH)
    pl.semaphore_wait(barrier, n_mp - 1)
    for load in loads:
        load.wait()

    def to_rows(q, k):
        return pltpu.make_async_remote_copy(
            src_ref=agg_out.at[q, k - 1],
            dst_ref=agg_in.at[q, k],
            send_sem=send_a.at[q, k - 1],
            recv_sem=recv_a.at[q, k - 1],
            device_id={"mp": (me + k) % n_mp},
            device_id_type=MESH,
        )

    def to_columns(q, k):
        return pltpu.make_async_remote_copy(
            src_ref=res_out.at[q, k - 1],
            dst_ref=out.at[pl.ds(pl.multiple_of((me * CHUNKS + q) * rows, rows), rows)],
            send_sem=send_b.at[q, k - 1],
            recv_sem=recv_b.at[q, k - 1],
            device_id={"mp": (me + k) % n_mp},
            device_id_type=MESH,
        )

    def aggregate(q, k, dst):
        first = ((me + k) % n_mp) * per_dev + q * per_chunk

        def one(i, carry):
            t = first + i
            lhs = jnp.concatenate([tiles[t, j] for j in range(kb)], axis=1)
            rhs = jnp.concatenate([srcs[src_idx[t * kb + j]] for j in range(kb)], axis=0)
            block = jnp.dot(lhs, rhs, preferred_element_type=jnp.float32)
            dst[pl.ds(pl.multiple_of(i * BLK, BLK), BLK), :] = block.astype(dst.dtype)
            return carry

        lax.fori_loop(0, per_chunk, one, 0)

    def multiply(q):
        for k in range(1, n_mp):
            to_rows(q, k).wait_recv()
        for n in list(range(1, n_mp)) + [0]:
            part = bias[(n_mp - n) % n_mp] + jnp.zeros((rows, 1), jnp.float32)
            for k in range(n_mp):
                part = part + jnp.dot(
                    agg_in[q, k], wts[k, (me + n) % n_mp], preferred_element_type=jnp.float32
                )
            part = jnp.maximum(part, 0.0).astype(out.dtype)
            if n:
                res_out[q, n - 1] = part
                to_columns(q, n).start()
            else:
                out[pl.ds(pl.multiple_of((me * CHUNKS + q) * rows, rows), rows), :] = part

    for q in range(CHUNKS + 1):
        if q < CHUNKS:
            for k in (2, 1, 3, 0):
                if k:
                    aggregate(q, k, agg_out.at[q, k - 1])
                    to_rows(q, k).start()
                else:
                    aggregate(q, k, agg_in.at[q, 0])
        if q:
            multiply(q - 1)
    for q in range(CHUNKS):
        for k in range(1, n_mp):
            to_rows(q, k).wait_send()
            to_columns(q, k).wait()


def layer(src_idx, own, partner, pulled, adj, wts, bias):
    n_mp = wts.shape[0]
    tb, kb = adj.shape[:2]
    width = own.shape[-1]
    n_src = own.shape[0] + partner.shape[0] + pulled.shape[0]
    rows = tb // n_mp // CHUNKS * BLK
    any_spec = pl.BlockSpec(memory_space=pl.ANY)
    vmem_spec = pl.BlockSpec(memory_space=pltpu.VMEM)

    def kernel(*refs):
        layer_kernel(n_mp, *refs)

    return pl.pallas_call(
        kernel,
        out_shape=jax.ShapeDtypeStruct((tb * BLK, width), jnp.bfloat16),
        in_specs=[pl.BlockSpec(memory_space=pltpu.SMEM)] + [any_spec] * 4 + [vmem_spec] * 2,
        out_specs=vmem_spec,
        scratch_shapes=[
            pltpu.VMEM((n_src + 1, BLK, width), jnp.bfloat16),
            pltpu.VMEM(adj.shape, jnp.bfloat16),
            pltpu.VMEM((CHUNKS, n_mp - 1, rows, width), jnp.bfloat16),
            pltpu.VMEM((CHUNKS, n_mp, rows, width), jnp.bfloat16),
            pltpu.VMEM((CHUNKS, n_mp - 1, rows, width), jnp.bfloat16),
            pltpu.SemaphoreType.DMA((4,)),
        ]
        + [pltpu.SemaphoreType.DMA((CHUNKS, n_mp - 1))] * 4,
        compiler_params=pltpu.CompilerParams(
            collective_id=0, has_side_effects=True, vmem_limit_bytes=44 << 20
        ),
        name="layer",
    )(src_idx, own, partner, pulled, adj, wts, bias)


def pull_kernel(block_ids, hist, out, held, picked, load_sem, send_sems, recv_sems):
    y, core = lax.axis_index("y"), lax.axis_index("core")
    me = y * NC + core
    per_peer = picked.shape[1]

    load = pltpu.make_async_copy(hist, held, load_sem.at[0])
    load.start()
    barrier = pltpu.get_barrier_semaphore()
    peers = [(dy, dc) for dy in (2, 1, 3, 0) for dc in range(NC)]
    peers.remove((0, 0))
    for dy, dc in peers:
        pl.semaphore_signal(
            barrier, inc=1, device_id={"y": (y + dy) % NY, "core": (core + dc) % NC},
            device_id_type=MESH,
        )
    pl.semaphore_wait(barrier, len(peers))
    load.wait()

    mine = out.at[pl.ds(me * per_peer, per_peer)]
    copies = []
    for n, (dy, dc) in enumerate(peers + [(0, 0)]):
        to_y, to_core = (y + dy) % NY, (core + dc) % NC
        first = (to_y * NC + to_core) * per_peer

        def pick(s, carry):
            picked[n, s] = held[block_ids[first + s]]
            return carry

        lax.fori_loop(0, per_peer, pick, 0)
        if dy or dc:
            copy = pltpu.make_async_remote_copy(
                src_ref=picked.at[n],
                dst_ref=mine,
                send_sem=send_sems.at[n],
                recv_sem=recv_sems.at[n],
                device_id={"y": to_y, "core": to_core},
                device_id_type=MESH,
            )
        else:
            copy = pltpu.make_async_copy(picked.at[n], mine, load_sem.at[0])
        copy.start()
        copies.append(copy)
    for copy in copies:
        copy.wait()


def pull(block_ids, hist):
    n_peers = NY * NC
    total = block_ids.shape[0]
    width = hist.shape[-1]
    any_spec = pl.BlockSpec(memory_space=pl.ANY)
    return pl.pallas_call(
        pull_kernel,
        out_shape=jax.ShapeDtypeStruct((total, BLK, width), jnp.bfloat16),
        in_specs=[pl.BlockSpec(memory_space=pltpu.SMEM), any_spec],
        out_specs=any_spec,
        scratch_shapes=[
            pltpu.VMEM(hist.shape, jnp.bfloat16),
            pltpu.VMEM((n_peers, total // n_peers, BLK, width), jnp.bfloat16),
            pltpu.SemaphoreType.DMA((1,)),
            pltpu.SemaphoreType.DMA((n_peers - 1,)),
            pltpu.SemaphoreType.DMA((n_peers - 1,)),
        ],
        compiler_params=pltpu.CompilerParams(
            collective_id=1, has_side_effects=True, vmem_limit_bytes=60 << 20
        ),
        cost_estimate=pl.CostEstimate(flops=0, bytes_accessed=256 << 20, transcendentals=0),
        name="pull",
    )(block_ids, hist)


def xor_permute(value, axes, size, which):
    def branch(m):
        if m == 0:
            return lambda v: v
        pairs = [(s, s ^ m) for s in range(size)]
        return lambda v: lax.ppermute(v, axes, pairs)

    return lax.switch(which, [branch(m) for m in range(size)], value)


def from_all(value, axis):
    n = lax.axis_size(axis)
    moved = [lax.ppermute(value, axis, [(s, (s + k) % n) for s in range(n)]) for k in range(1, n)]
    return jnp.stack([value] + moved)


def per_device(
    features, history, adj_values, adj_sources, pull_list, pull_count, partner_mask, weight, bias
):
    row_count, width = features.shape
    row_blocks = row_count // BLK
    cap = pull_list.shape[-1]
    hist_blocks = history.shape[0] // BLK
    mask = partner_mask[0]
    n_mp = lax.axis_size("mp")
    yc_mask = (mask >> 4) * NC + (mask & 1)
    z_mask = (mask >> 1) & (NZ - 1)

    hist_z = lax.all_gather(history, "z", axis=0, tiled=True)
    wanted = pull_list[0].reshape(NY, NZ, NC, cap).transpose(0, 2, 1, 3).reshape(NY * NC, NZ, cap)
    asked = lax.all_to_all(wanted, ("y", "core"), split_axis=0, concat_axis=0, tiled=True)
    block_ids = asked + jnp.arange(NZ, dtype=jnp.int32)[None, :, None] * hist_blocks

    wts = from_all(weight.reshape(width, n_mp, width).transpose(1, 0, 2), "mp")
    biases = from_all(bias.reshape(1, width), "mp")

    half_way = xor_permute(features, ("y", "core"), NY * NC, yc_mask)
    hist_z, half_way, block_ids, wts, biases = lax.optimization_barrier(
        (hist_z, half_way, block_ids, wts, biases)
    )

    def pull_beside(m):
        def branch(rows, ids, hist):
            if m:
                rows = lax.ppermute(rows, "z", [(s, s ^ m) for s in range(NZ)])
            return rows, pull(ids, hist)

        return branch

    partner_rows, pulled = lax.switch(
        z_mask,
        [pull_beside(m) for m in range(NZ)],
        half_way,
        block_ids.reshape(-1),
        hist_z.reshape(NZ * hist_blocks, BLK, width),
    )

    slot_no = jnp.maximum(adj_sources - 2 * row_blocks, 0)
    owner, slot = slot_no // cap, slot_no % cap
    oy, oz, oc = owner // (NZ * NC), (owner // NC) % NZ, owner % NC
    moved = ((oy * NC + oc) * NZ + oz) * cap + slot
    alive = (jnp.arange(cap)[None, :] < pull_count[0][:, None]).reshape(-1)
    n_pulled = NY * NZ * NC * cap
    pulled_src = 2 * row_blocks + jnp.where(alive[slot_no], moved, n_pulled)
    src_idx = jnp.where(adj_sources >= 2 * row_blocks, pulled_src, adj_sources)

    return layer(
        src_idx.reshape(-1),
        features.reshape(row_blocks, BLK, width),
        partner_rows.reshape(row_blocks, BLK, width),
        pulled,
        adj_values,
        wts,
        biases,
    )


def solution(mesh):
    n_mp = mesh.devices.shape[1]
    fine = Mesh(mesh.devices.reshape(NY, NZ, NC, n_mp), ("y", "z", "core", "mp"))
    dp = ("y", "z", "core")
    in_specs = (
        P(dp, "mp"),
        P(dp, "mp"),
        P(dp, None, None, None),
        P(dp, None),
        P(dp, None, None),
        P(dp, None),
        P(),
        P("mp", None),
        P("mp"),
    )
    return jax.shard_map(
        per_device, mesh=fine, in_specs=in_specs, out_specs=P(dp, "mp"), check_vma=False
    )
```

```python
import jax
import jax.numpy as jnp
from jax import lax
from jax.experimental import pallas as pl
from jax.experimental.pallas import tpu as pltpu
from jax.sharding import Mesh, PartitionSpec as P

NY, NZ, NC = 4, 8, 2
BLK = 128
CHUNKS = 4
PIECES = 2
DP = ("y", "z", "core")
MESH = pl.DeviceIdType.MESH


def layer_kernel(
    n_mp, src_idx, own, partner, pulled, adj, my_bias, *refs
):
    wts, refs = refs[:n_mp], refs[n_mp:]
    (
        out, srcs, tiles, bias, agg_out, agg_in, res_out,
        load_sem, bias_send, bias_recv, send_a, recv_a, send_b, recv_b,
    ) = refs
    me = lax.axis_index("mp")
    tb, kb = adj.shape[:2]
    nb, n_pulled = own.shape[0], pulled.shape[0]
    n_src = 2 * nb + n_pulled
    per_dev = tb // n_mp
    per_chunk = per_dev // CHUNKS
    rows = per_chunk * BLK

    loads = [
        pltpu.make_async_copy(own, srcs.at[pl.ds(0, nb)], load_sem.at[0]),
        pltpu.make_async_copy(partner, srcs.at[pl.ds(nb, nb)], load_sem.at[1]),
        pltpu.make_async_copy(pulled, srcs.at[pl.ds(2 * nb, n_pulled)], load_sem.at[2]),
        pltpu.make_async_copy(adj, tiles, load_sem.at[3]),
    ]
    for load in loads:
        load.start()
    srcs[n_src] = jnp.zeros(srcs.shape[1:], srcs.dtype)

    barrier = pltpu.get_barrier_semaphore()
    for k in range(1, n_mp):
        pl.semaphore_signal(barrier, inc=1, device_id={"mp": (me + k) % n_mp}, device_id_type=MESH)
    pl.semaphore_wait(barrier, n_mp - 1)

    def to_bias(k):
        return pltpu.make_async_remote_copy(
            src_ref=my_bias,
            dst_ref=bias.at[k],
            send_sem=bias_send.at[k - 1],
            recv_sem=bias_recv.at[k - 1],
            device_id={"mp": (me + k) % n_mp},
            device_id_type=MESH,
        )

    for k in range(1, n_mp):
        to_bias(k).start()
    bias[0] = my_bias[...]
    for load in loads:
        load.wait()
    for k in range(1, n_mp):
        to_bias(k).wait()

    def to_rows(q, k):
        return pltpu.make_async_remote_copy(
            src_ref=agg_out.at[q, k - 1],
            dst_ref=agg_in.at[q, k],
            send_sem=send_a.at[q, k - 1],
            recv_sem=recv_a.at[q, k - 1],
            device_id={"mp": (me + k) % n_mp},
            device_id_type=MESH,
        )

    def to_columns(q, k):
        return pltpu.make_async_remote_copy(
            src_ref=res_out.at[q, k - 1],
            dst_ref=out.at[pl.ds(pl.multiple_of((me * CHUNKS + q) * rows, rows), rows)],
            send_sem=send_b.at[q, k - 1],
            recv_sem=recv_b.at[q, k - 1],
            device_id={"mp": (me + k) % n_mp},
            device_id_type=MESH,
        )

    def aggregate(q, k, dst):
        first = ((me + k) % n_mp) * per_dev + q * per_chunk

        def one(i, carry):
            t = first + i
            lhs = jnp.concatenate([tiles[t, j] for j in range(kb)], axis=1)
            rhs = jnp.concatenate([srcs[src_idx[t * kb + j]] for j in range(kb)], axis=0)
            block = jnp.dot(lhs, rhs, preferred_element_type=jnp.float32)
            dst[pl.ds(pl.multiple_of(i * BLK, BLK), BLK), :] = block.astype(dst.dtype)
            return carry

        lax.fori_loop(0, per_chunk, one, 0)

    def multiply(q):
        for k in range(1, n_mp):
            to_rows(q, k).wait_recv()
        for n in list(range(1, n_mp)) + [0]:
            part = bias[(n_mp - n) % n_mp] + jnp.zeros((rows, 1), jnp.float32)
            for k in range(n_mp):
                part = part + jnp.dot(
                    agg_in[q, k], wts[k][(me + n) % n_mp], preferred_element_type=jnp.float32
                )
            part = jnp.maximum(part, 0.0).astype(out.dtype)
            if n:
                res_out[q, n - 1] = part
                to_columns(q, n).start()
            else:
                out[pl.ds(pl.multiple_of((me * CHUNKS + q) * rows, rows), rows), :] = part

    def chunk(q, carry):
        @pl.when(q < CHUNKS)
        def _():
            for k in (2, 1, 3):
                aggregate(q, k, agg_out.at[q, k - 1])
                to_rows(q, k).start()
            aggregate(q, 0, agg_in.at[q, 0])

        @pl.when(q > 0)
        def _():
            multiply(q - 1)

        return carry

    lax.fori_loop(0, CHUNKS + 1, chunk, 0)

    def finish(q, carry):
        for k in range(1, n_mp):
            to_rows(q, k).wait_send()
            to_columns(q, k).wait()
        return carry

    lax.fori_loop(0, CHUNKS, finish, 0)


def layer(src_idx, own, partner, pulled, adj, wts, bias):
    n_mp = len(wts)
    tb, kb = adj.shape[:2]
    width = own.shape[-1]
    n_src = own.shape[0] + partner.shape[0] + pulled.shape[0]
    rows = tb // n_mp // CHUNKS * BLK
    any_spec = pl.BlockSpec(memory_space=pl.ANY)
    vmem_spec = pl.BlockSpec(memory_space=pltpu.VMEM)

    def kernel(*refs):
        layer_kernel(n_mp, *refs)

    return pl.pallas_call(
        kernel,
        out_shape=jax.ShapeDtypeStruct((tb * BLK, width), jnp.bfloat16),
        in_specs=[pl.BlockSpec(memory_space=pltpu.SMEM)] + [any_spec] * 4 + [vmem_spec] * (1 + n_mp),
        out_specs=vmem_spec,
        scratch_shapes=[
            pltpu.VMEM((n_src + 1, BLK, width), jnp.bfloat16),
            pltpu.VMEM(adj.shape, jnp.bfloat16),
            pltpu.VMEM((n_mp,) + bias.shape, jnp.float32),
            pltpu.VMEM((CHUNKS, n_mp - 1, rows, width), jnp.bfloat16),
            pltpu.VMEM((CHUNKS, n_mp, rows, width), jnp.bfloat16),
            pltpu.VMEM((CHUNKS, n_mp - 1, rows, width), jnp.bfloat16),
            pltpu.SemaphoreType.DMA((4,)),
            pltpu.SemaphoreType.DMA((n_mp - 1,)),
            pltpu.SemaphoreType.DMA((n_mp - 1,)),
        ]
        + [pltpu.SemaphoreType.DMA((CHUNKS, n_mp - 1))] * 4,
        compiler_params=pltpu.CompilerParams(
            collective_id=0, has_side_effects=True, vmem_limit_bytes=44 << 20
        ),
        name="layer",
    )(src_idx, own, partner, pulled, adj, bias, *wts)


def pull_kernel(block_ids, hist, out, *scratch):
    shards = scratch[:NZ]
    picked, load_sem, ring_send, ring_recv, send_sems, recv_sems = scratch[NZ:]
    y, z, core = lax.axis_index("y"), lax.axis_index("z"), lax.axis_index("core")
    cap = picked.shape[2]
    piece = hist.shape[0] // PIECES
    me = y * NC + core
    n_peers = NY * NC - 1

    def peer(n):
        at = 3 * (n + 1) % (NC * NY)
        return (y + at // NC) % NY, (core + at % NC) % NC

    load = pltpu.make_async_copy(hist, shards[0], load_sem.at[NZ])
    load.start()
    barrier = pltpu.get_barrier_semaphore()
    for n in range(n_peers):
        to_y, to_core = peer(n)
        pl.semaphore_signal(
            barrier, inc=1, device_id={"y": to_y, "core": to_core}, device_id_type=MESH
        )
    for dz in (1, NZ - 1):
        pl.semaphore_signal(barrier, inc=1, device_id={"z": (z + dz) % NZ}, device_id_type=MESH)
    pl.semaphore_wait(barrier, n_peers + 2)

    def hop(up, s, p):
        src, dst = (s - 1, s) if up else ((NZ - s + 1) % NZ, NZ - s)
        part = pl.ds(p * piece, piece)
        return pltpu.make_async_remote_copy(
            src_ref=(shards[src] if src else hist).at[part],
            dst_ref=shards[dst].at[part],
            send_sem=ring_send.at[0 if up else 1, s - 1, p],
            recv_sem=ring_recv.at[0 if up else 1, s - 1, p],
            device_id={"z": (z + (1 if up else NZ - 1)) % NZ},
            device_id_type=MESH,
        )

    half = NZ // 2
    hops = [
        [(up, p) for p in range(PIECES) for up in (True, False)
         if s < half or (p < PIECES // 2) == up]
        for s in range(half + 1)
    ]

    def rows(r):
        return out.at[pl.ds((me * NZ + (z + NZ - r) % NZ) * cap, cap)]

    def give(r, n):
        to_y, to_core = peer(n)
        return pltpu.make_async_remote_copy(
            src_ref=picked.at[r, n],
            dst_ref=rows(r),
            send_sem=send_sems.at[r, n],
            recv_sem=recv_sems.at[r, n],
            device_id={"y": to_y, "core": to_core},
            device_id_type=MESH,
        )

    def keep(r):
        return pltpu.make_async_copy(picked.at[r, n_peers], rows(r), load_sem.at[r])

    def serve(r):
        def one(n, carry):
            to_y, to_core = peer(n)
            first = ((to_y * NC + to_core) * NZ + (z + NZ - r) % NZ) * cap
            for slot in range(cap):
                picked[r, n, slot] = shards[r][block_ids[first + slot]]

            @pl.when(n < n_peers)
            def _():
                give(r, n).start()

            return carry

        lax.fori_loop(0, n_peers + 1, one, 0)
        keep(r).start()

    for up, p in hops[1]:
        hop(up, 1, p).start()
    load.wait()
    serve(0)
    for s in range(1, half + 1):
        for up, p in hops[s]:
            hop(up, s, p).wait_recv()
            if s < half and (up, p) in hops[s + 1]:
                hop(up, s + 1, p).start()
        serve(s)
        if s < half:
            serve(NZ - s)
    for s in range(1, half + 1):
        for up, p in hops[s]:
            hop(up, s, p).wait_send()
    def finish(r, carry):
        def one(n, inner):
            give(r, n).wait()
            return inner

        lax.fori_loop(0, n_peers, one, 0)
        keep(r).wait()
        return carry

    lax.fori_loop(0, NZ, finish, 0)


def pull(block_ids, hist):
    n_peers = NY * NC
    total = block_ids.shape[0]
    cap = total // n_peers // NZ
    blocks, width = hist.shape[0], hist.shape[-1]
    any_spec = pl.BlockSpec(memory_space=pl.ANY)
    return pl.pallas_call(
        pull_kernel,
        out_shape=jax.ShapeDtypeStruct((total, BLK, width), jnp.bfloat16),
        in_specs=[pl.BlockSpec(memory_space=pltpu.SMEM), any_spec],
        out_specs=any_spec,
        scratch_shapes=[pltpu.VMEM(hist.shape, jnp.bfloat16)] * NZ
        + [
            pltpu.VMEM((NZ, n_peers, cap, BLK, width), jnp.bfloat16),
            pltpu.SemaphoreType.DMA((NZ + 1,)),
            pltpu.SemaphoreType.DMA((2, NZ // 2, PIECES)),
            pltpu.SemaphoreType.DMA((2, NZ // 2, PIECES)),
            pltpu.SemaphoreType.DMA((NZ, n_peers - 1)),
            pltpu.SemaphoreType.DMA((NZ, n_peers - 1)),
        ],
        compiler_params=pltpu.CompilerParams(
            collective_id=1, has_side_effects=True, vmem_limit_bytes=60 << 20
        ),
        cost_estimate=pl.CostEstimate(flops=0, bytes_accessed=256 << 20, transcendentals=0),
        name="pull",
    )(block_ids, hist)


def from_all(value, axis):
    n = lax.axis_size(axis)
    moved = [lax.ppermute(value, axis, [(s, (s + k) % n) for s in range(n)]) for k in range(1, n)]
    return [value] + moved


def per_device(
    features, history, adj_values, adj_sources, pull_list, pull_count, partner_mask, weight, bias
):
    row_count, width = features.shape
    row_blocks = row_count // BLK
    cap = pull_list.shape[-1]
    hist_blocks = history.shape[0] // BLK
    mask = partner_mask[0]
    n_mp = lax.axis_size("mp")
    wanted = pull_list[0].reshape(NY, NZ, NC, cap).transpose(0, 2, 1, 3).reshape(NY * NC, NZ, cap)
    asked = lax.all_to_all(wanted, ("y", "core"), split_axis=0, concat_axis=0, tiled=True)

    wts = from_all(weight.reshape(width, n_mp, width).transpose(1, 0, 2), "mp")

    swapped = lax.cond(
        mask % NC == 1,
        lambda rows: lax.ppermute(rows, "core", [(s, NC - 1 - s) for s in range(NC)]),
        lambda rows: rows,
        features,
    )

    slot_no = jnp.maximum(adj_sources - 2 * row_blocks, 0)
    owner, slot = slot_no // cap, slot_no % cap
    oy, oz, oc = owner // (NZ * NC), (owner // NC) % NZ, owner % NC
    moved = ((oy * NC + oc) * NZ + oz) * cap + slot
    alive = (jnp.arange(cap)[None, :] < pull_count[0][:, None]).reshape(-1)
    n_pulled = NY * NZ * NC * cap
    pulled_src = 2 * row_blocks + jnp.where(alive[slot_no], moved, n_pulled)
    src_idx = jnp.where(adj_sources >= 2 * row_blocks, pulled_src, adj_sources)
    asked, src_idx = lax.optimization_barrier((asked.reshape(-1), src_idx.reshape(-1)))

    def pull_beside(m):
        def branch(rows, ids, hist):
            if m:
                rows = lax.ppermute(rows, ("y", "z"), [(s, s ^ m) for s in range(NY * NZ)])
            return rows, pull(ids, hist)

        return branch

    partner_rows, pulled = lax.switch(
        mask // NC,
        [pull_beside(m) for m in range(NY * NZ)],
        swapped,
        asked,
        history.reshape(hist_blocks, BLK, width),
    )

    return layer(
        src_idx,
        features.reshape(row_blocks, BLK, width),
        partner_rows.reshape(row_blocks, BLK, width),
        pulled,
        adj_values,
        wts,
        bias.reshape(1, width),
    )


def solution(mesh):
    n_mp = mesh.devices.shape[1]
    fine = Mesh(mesh.devices.reshape(NY, NZ, NC, n_mp), ("y", "z", "core", "mp"))
    in_specs = (
        P(DP, "mp"),
        P(DP, "mp"),
        P(DP, None, None, None),
        P(DP, None),
        P(DP, None, None),
        P(DP, None),
        P(),
        P("mp", None),
        P("mp"),
    )
    return jax.shard_map(
        per_device, mesh=fine, in_specs=in_specs, out_specs=P(DP, "mp"), check_vma=False
    )
```

```python
import jax
import jax.numpy as jnp
from jax import lax
from jax.experimental import pallas as pl
from jax.experimental.pallas import tpu as pltpu
from jax.sharding import Mesh, PartitionSpec as P

NY, NZ, NC = 4, 8, 2
BLK = 128
CHUNKS = 4
DP = ("y", "z", "core")
MESH = pl.DeviceIdType.MESH


def layer_kernel(
    n_mp, src_idx, own, partner, pulled, adj, unread, my_bias, *refs
):
    wts, refs = refs[:n_mp], refs[n_mp:]
    (
        out, srcs, tiles, bias, agg_out, agg_in, res_out,
        load_sem, bias_send, bias_recv, send_a, recv_a, send_b, recv_b,
    ) = refs
    me = lax.axis_index("mp")
    per_chunk, kb = adj.shape[2:4]
    nb, n_pulled = own.shape[0], pulled.shape[0]
    n_src = 2 * nb + n_pulled
    rows = per_chunk * BLK

    def adj_load(q):
        return pltpu.make_async_copy(adj.at[:, q], tiles.at[:, q], load_sem.at[3 + q])

    loads = [
        pltpu.make_async_copy(own, srcs.at[pl.ds(0, nb)], load_sem.at[0]),
        pltpu.make_async_copy(partner, srcs.at[pl.ds(nb, nb)], load_sem.at[1]),
        pltpu.make_async_copy(pulled, srcs.at[pl.ds(2 * nb, n_pulled)], load_sem.at[2]),
    ]
    for load in loads:
        load.start()
    for q in range(CHUNKS):
        adj_load(q).start()
    srcs[n_src] = jnp.zeros(srcs.shape[1:], srcs.dtype)

    barrier = pltpu.get_barrier_semaphore()
    for k in range(1, n_mp):
        pl.semaphore_signal(barrier, inc=1, device_id={"mp": (me + k) % n_mp}, device_id_type=MESH)
    pl.semaphore_wait(barrier, n_mp - 1)

    def to_bias(k):
        return pltpu.make_async_remote_copy(
            src_ref=my_bias,
            dst_ref=bias.at[k],
            send_sem=bias_send.at[k - 1],
            recv_sem=bias_recv.at[k - 1],
            device_id={"mp": (me + k) % n_mp},
            device_id_type=MESH,
        )

    for k in range(1, n_mp):
        to_bias(k).start()
    bias[0] = my_bias[...]
    for load in loads:
        load.wait()
    for k in range(1, n_mp):
        to_bias(k).wait()

    def to_rows(q, k):
        return pltpu.make_async_remote_copy(
            src_ref=agg_out.at[q, k - 1],
            dst_ref=agg_in.at[q, k],
            send_sem=send_a.at[q, k - 1],
            recv_sem=recv_a.at[q, k - 1],
            device_id={"mp": (me + k) % n_mp},
            device_id_type=MESH,
        )

    def to_columns(q, k):
        return pltpu.make_async_remote_copy(
            src_ref=res_out.at[q, k - 1],
            dst_ref=out.at[pl.ds(pl.multiple_of((me * CHUNKS + q) * rows, rows), rows)],
            send_sem=send_b.at[q, k - 1],
            recv_sem=recv_b.at[q, k - 1],
            device_id={"mp": (me + k) % n_mp},
            device_id_type=MESH,
        )

    def aggregate(q, k, dst):
        dev = (me + k) % n_mp

        def one(i, carry):
            first = ((dev * CHUNKS + q) * per_chunk + i) * kb
            lhs = jnp.concatenate([tiles[dev, q, i, j] for j in range(kb)], axis=1)
            rhs = jnp.concatenate([srcs[src_idx[first + j]] for j in range(kb)], axis=0)
            block = jnp.dot(lhs, rhs, preferred_element_type=jnp.float32)
            dst[pl.ds(pl.multiple_of(i * BLK, BLK), BLK), :] = block.astype(dst.dtype)
            return carry

        lax.fori_loop(0, per_chunk, one, 0)

    def multiply(q):
        for k in range(1, n_mp):
            to_rows(q, k).wait_recv()
        for n in list(range(1, n_mp)) + [0]:
            part = bias[(n_mp - n) % n_mp] + jnp.zeros((rows, 1), jnp.float32)
            for k in range(n_mp):
                part = part + jnp.dot(
                    agg_in[q, k], wts[k][(me + n) % n_mp], preferred_element_type=jnp.float32
                )
            part = jnp.maximum(part, 0.0).astype(out.dtype)
            if n:
                res_out[q, n - 1] = part
                to_columns(q, n).start()
            else:
                out[pl.ds(pl.multiple_of((me * CHUNKS + q) * rows, rows), rows), :] = part

    for q in range(CHUNKS + 1):
        if q < CHUNKS:
            adj_load(q).wait()
            for k in (2, 1, 3):
                aggregate(q, k, agg_out.at[q, k - 1])
                to_rows(q, k).start()
            aggregate(q, 0, agg_in.at[q, 0])
        if q:
            multiply(q - 1)
    for q in range(CHUNKS):
        for k in range(1, n_mp):
            to_rows(q, k).wait_send()
            to_columns(q, k).wait()


def layer(src_idx, own, partner, pulled, adj, unread, wts, bias):
    n_mp = len(wts)
    tb, kb = adj.shape[:2]
    adj = adj.reshape(n_mp, CHUNKS, tb // n_mp // CHUNKS, kb, BLK, BLK)
    width = own.shape[-1]
    n_src = own.shape[0] + partner.shape[0] + pulled.shape[0]
    rows = tb // n_mp // CHUNKS * BLK
    any_spec = pl.BlockSpec(memory_space=pl.ANY)
    vmem_spec = pl.BlockSpec(memory_space=pltpu.VMEM)

    def kernel(*refs):
        layer_kernel(n_mp, *refs)

    return pl.pallas_call(
        kernel,
        out_shape=jax.ShapeDtypeStruct((tb * BLK, width), jnp.bfloat16),
        in_specs=[pl.BlockSpec(memory_space=pltpu.SMEM)] + [any_spec] * 5 + [vmem_spec] * (1 + n_mp),
        out_specs=vmem_spec,
        scratch_shapes=[
            pltpu.VMEM((n_src + 1, BLK, width), jnp.bfloat16),
            pltpu.VMEM(adj.shape, jnp.bfloat16),
            pltpu.VMEM((n_mp,) + bias.shape, jnp.float32),
            pltpu.VMEM((CHUNKS, n_mp - 1, rows, width), jnp.bfloat16),
            pltpu.VMEM((CHUNKS, n_mp, rows, width), jnp.bfloat16),
            pltpu.VMEM((CHUNKS, n_mp - 1, rows, width), jnp.bfloat16),
            pltpu.SemaphoreType.DMA((3 + CHUNKS,)),
            pltpu.SemaphoreType.DMA((n_mp - 1,)),
            pltpu.SemaphoreType.DMA((n_mp - 1,)),
        ]
        + [pltpu.SemaphoreType.DMA((CHUNKS, n_mp - 1))] * 4,
        compiler_params=pltpu.CompilerParams(
            collective_id=0, has_side_effects=True, vmem_limit_bytes=44 << 20
        ),
        name="layer",
    )(src_idx, own, partner, pulled, adj, unread, bias, *wts)


def pull_kernel(block_ids, hist, out, *scratch):
    shards = scratch[:NZ]
    picked, load_sem, keep_sem, send_sems, recv_sems = scratch[NZ:]
    y, core = lax.axis_index("y"), lax.axis_index("core")
    cap = picked.shape[2]
    me = y * NC + core
    n_peers = NY * NC - 1

    def peer(n):
        at = 3 * (n + 1) % (NC * NY)
        return (y + at // NC) % NY, (core + at % NC) % NC

    loads = [pltpu.make_async_copy(hist.at[r], shards[r], load_sem.at[r]) for r in range(NZ)]
    for load in loads:
        load.start()
    barrier = pltpu.get_barrier_semaphore()
    for n in range(n_peers):
        to_y, to_core = peer(n)
        pl.semaphore_signal(
            barrier, inc=1, device_id={"y": to_y, "core": to_core}, device_id_type=MESH
        )
    pl.semaphore_wait(barrier, n_peers)

    def rows(r):
        return out.at[pl.ds((me * NZ + r) * cap, cap)]

    def give(r, n):
        to_y, to_core = peer(n)
        return pltpu.make_async_remote_copy(
            src_ref=picked.at[r, n],
            dst_ref=rows(r),
            send_sem=send_sems.at[r, n],
            recv_sem=recv_sems.at[r, n],
            device_id={"y": to_y, "core": to_core},
            device_id_type=MESH,
        )

    def keep(r):
        return pltpu.make_async_copy(picked.at[r, n_peers], rows(r), keep_sem.at[r])

    for r in range(NZ):
        loads[r].wait()

        def one(n, carry):
            to_y, to_core = peer(n)
            first = ((to_y * NC + to_core) * NZ + r) * cap
            for slot in range(cap):
                picked[r, n, slot] = shards[r][block_ids[first + slot]]

            @pl.when(n < n_peers)
            def _():
                give(r, n).start()

            return carry

        lax.fori_loop(0, n_peers + 1, one, 0)
        keep(r).start()

    def finish(r, carry):
        def one(n, inner):
            give(r, n).wait()
            return inner

        lax.fori_loop(0, n_peers, one, 0)
        keep(r).wait()
        return carry

    lax.fori_loop(0, NZ, finish, 0)


def pull(block_ids, hist):
    n_peers = NY * NC
    total = block_ids.shape[0]
    cap = total // n_peers // NZ
    width = hist.shape[-1]
    any_spec = pl.BlockSpec(memory_space=pl.ANY)
    return pl.pallas_call(
        pull_kernel,
        out_shape=jax.ShapeDtypeStruct((total, BLK, width), jnp.bfloat16),
        in_specs=[pl.BlockSpec(memory_space=pltpu.SMEM), any_spec],
        out_specs=any_spec,
        scratch_shapes=[pltpu.VMEM(hist.shape[1:], jnp.bfloat16)] * NZ
        + [
            pltpu.VMEM((NZ, n_peers, cap, BLK, width), jnp.bfloat16),
            pltpu.SemaphoreType.DMA((NZ,)),
            pltpu.SemaphoreType.DMA((NZ,)),
            pltpu.SemaphoreType.DMA((NZ, n_peers - 1)),
            pltpu.SemaphoreType.DMA((NZ, n_peers - 1)),
        ],
        compiler_params=pltpu.CompilerParams(
            collective_id=1, has_side_effects=True, vmem_limit_bytes=60 << 20
        ),
        cost_estimate=pl.CostEstimate(flops=0, bytes_accessed=256 << 20, transcendentals=0),
        name="pull",
    )(block_ids, hist)


def xor_permute(value, axes, size, which):
    def branch(m):
        if m == 0:
            return lambda v: v
        pairs = [(s, s ^ m) for s in range(size)]
        return lambda v: lax.ppermute(v, axes, pairs)

    return lax.switch(which, [branch(m) for m in range(size)], value)


def from_all(value, axis):
    n = lax.axis_size(axis)
    moved = [lax.ppermute(value, axis, [(s, (s + k) % n) for s in range(n)]) for k in range(1, n)]
    return [value] + moved


def per_device(
    features, history, adj_values, adj_sources, pull_list, pull_count, partner_mask, weight, bias
):
    row_count, width = features.shape
    row_blocks = row_count // BLK
    cap = pull_list.shape[-1]
    hist_blocks = history.shape[0] // BLK
    mask = partner_mask[0]
    n_mp = lax.axis_size("mp")
    yc_mask = (mask >> 4) * NC + (mask & 1)
    z_mask = (mask >> 1) & (NZ - 1)

    hist_z = lax.all_gather(history, "z", axis=0, tiled=True)
    wanted = pull_list[0].reshape(NY, NZ, NC, cap).transpose(0, 2, 1, 3).reshape(NY * NC, NZ, cap)
    asked = lax.all_to_all(wanted, ("y", "core"), split_axis=0, concat_axis=0, tiled=True)

    wts = from_all(weight.reshape(width, n_mp, width).transpose(1, 0, 2), "mp")

    half_way = xor_permute(features, ("y", "core"), NY * NC, yc_mask)

    slot_no = jnp.maximum(adj_sources - 2 * row_blocks, 0)
    owner, slot = slot_no // cap, slot_no % cap
    oy, oz, oc = owner // (NZ * NC), (owner // NC) % NZ, owner % NC
    moved = ((oy * NC + oc) * NZ + oz) * cap + slot
    alive = (jnp.arange(cap)[None, :] < pull_count[0][:, None]).reshape(-1)
    n_pulled = NY * NZ * NC * cap
    pulled_src = 2 * row_blocks + jnp.where(alive[slot_no], moved, n_pulled)
    src_idx = jnp.where(adj_sources >= 2 * row_blocks, pulled_src, adj_sources)
    hist_z, half_way, asked, src_idx, *wts = lax.optimization_barrier(
        (hist_z, half_way, asked.reshape(-1), src_idx.reshape(-1), *wts)
    )

    def pull_beside(m):
        def branch(rows, ids, hist):
            if m:
                rows = lax.ppermute(rows, "z", [(s, s ^ m) for s in range(NZ)])
            return rows, pull(ids, hist)

        return branch

    partner_rows, pulled = lax.switch(
        z_mask,
        [pull_beside(m) for m in range(NZ)],
        half_way,
        asked,
        hist_z.reshape(NZ, hist_blocks, BLK, width),
    )

    return layer(
        src_idx,
        features.reshape(row_blocks, BLK, width),
        partner_rows.reshape(row_blocks, BLK, width),
        pulled,
        adj_values,
        half_way,
        wts,
        bias.reshape(1, width),
    )


def solution(mesh):
    n_mp = mesh.devices.shape[1]
    fine = Mesh(mesh.devices.reshape(NY, NZ, NC, n_mp), ("y", "z", "core", "mp"))
    in_specs = (
        P(DP, "mp"),
        P(DP, "mp"),
        P(DP, None, None, None),
        P(DP, None),
        P(DP, None, None),
        P(DP, None),
        P(),
        P("mp", None),
        P("mp"),
    )
    return jax.shard_map(
        per_device, mesh=fine, in_specs=in_specs, out_specs=P(DP, "mp"), check_vma=False
    )
```

```python
import jax
import jax.numpy as jnp
from jax import lax
from jax.experimental import pallas as pl
from jax.experimental.pallas import tpu as pltpu
from jax.sharding import Mesh, PartitionSpec as P

NY, NZ, NC = 4, 8, 2
BLK = 128
CHUNKS = 4
Z_PIECES = 4
Z_AHEAD = 2
Y_PIECES = 4
DP = ("y", "z", "core")
MESH = pl.DeviceIdType.MESH


def layer_kernel(
    n_mp, src_no, counts, own, partner, pulled, adj, unread, w_rows, my_bias,
    out, srcs, tiles, wts, bias, agg_out, agg_in, res_out,
    load_sem, w_sem, bias_send, bias_recv, send_a, recv_a, send_b, recv_b,
):
    me = lax.axis_index("mp")
    per_chunk, kb = adj.shape[2:4]
    nb, n_pulled = own.shape[0], pulled.shape[0]
    n_src = 2 * nb + n_pulled
    cap = n_pulled // (NY * NZ * NC)
    rows = per_chunk * BLK

    def adj_load(q):
        return pltpu.make_async_copy(adj.at[:, q], tiles.at[:, q], load_sem.at[3 + q])

    loads = [
        pltpu.make_async_copy(own, srcs.at[pl.ds(0, nb)], load_sem.at[0]),
        pltpu.make_async_copy(partner, srcs.at[pl.ds(nb, nb)], load_sem.at[1]),
        pltpu.make_async_copy(pulled, srcs.at[pl.ds(2 * nb, n_pulled)], load_sem.at[2]),
    ]
    for load in loads:
        load.start()
    for q in range(CHUNKS):
        adj_load(q).start()
    cols = own.shape[-1]
    w_loads = [
        pltpu.make_async_copy(
            w_rows.at[k, :, pl.ds(n * cols, cols)], wts.at[k, n], w_sem.at[k, n]
        )
        for k in range(n_mp)
        for n in range(n_mp)
    ]
    for load in w_loads:
        load.start()
    srcs[n_src] = jnp.zeros(srcs.shape[1:], srcs.dtype)

    barrier = pltpu.get_barrier_semaphore()
    for k in range(1, n_mp):
        pl.semaphore_signal(barrier, inc=1, device_id={"mp": (me + k) % n_mp}, device_id_type=MESH)
    pl.semaphore_wait(barrier, n_mp - 1)

    def to_bias(k):
        return pltpu.make_async_remote_copy(
            src_ref=my_bias,
            dst_ref=bias.at[k],
            send_sem=bias_send.at[k - 1],
            recv_sem=bias_recv.at[k - 1],
            device_id={"mp": (me + k) % n_mp},
            device_id_type=MESH,
        )

    for k in range(1, n_mp):
        to_bias(k).start()
    bias[0] = my_bias[...]
    for load in loads:
        load.wait()
    for k in range(1, n_mp):
        to_bias(k).wait()

    def to_rows(q, k):
        return pltpu.make_async_remote_copy(
            src_ref=agg_out.at[q, k - 1],
            dst_ref=agg_in.at[q, k],
            send_sem=send_a.at[q, k - 1],
            recv_sem=recv_a.at[q, k - 1],
            device_id={"mp": (me + k) % n_mp},
            device_id_type=MESH,
        )

    def to_columns(q, k):
        return pltpu.make_async_remote_copy(
            src_ref=res_out.at[q, k - 1],
            dst_ref=out.at[pl.ds(pl.multiple_of((me * CHUNKS + q) * rows, rows), rows)],
            send_sem=send_b.at[q, k - 1],
            recv_sem=recv_b.at[q, k - 1],
            device_id={"mp": (me + k) % n_mp},
            device_id_type=MESH,
        )

    def place(src):
        at = jnp.maximum(src - 2 * nb, 0)
        owner, slot = at // cap, at % cap
        oy, oz, oc = owner // (NZ * NC), owner // NC % NZ, owner % NC
        moved = 2 * nb + ((oy * NC + oc) * NZ + oz) * cap + slot
        moved = jnp.where(slot < counts[owner], moved, n_src)
        return jnp.where(src < 2 * nb, src, moved)

    def aggregate(q, k, dst):
        dev = (me + k) % n_mp

        def one(i, carry):
            first = ((dev * CHUNKS + q) * per_chunk + i) * kb
            lhs = jnp.concatenate([tiles[dev, q, i, j] for j in range(kb)], axis=1)
            rhs = jnp.concatenate([srcs[place(src_no[first + j])] for j in range(kb)], axis=0)
            block = jnp.dot(lhs, rhs, preferred_element_type=jnp.float32)
            dst[pl.ds(pl.multiple_of(i * BLK, BLK), BLK), :] = block.astype(dst.dtype)
            return carry

        lax.fori_loop(0, per_chunk, one, 0)

    def multiply(q):
        for k in range(1, n_mp):
            to_rows(q, k).wait_recv()
        for n in list(range(1, n_mp)) + [0]:
            part = bias[(n_mp - n) % n_mp] + jnp.zeros((rows, 1), jnp.float32)
            for k in range(n_mp):
                part = part + jnp.dot(
                    agg_in[q, k], wts[k, (me + n) % n_mp], preferred_element_type=jnp.float32
                )
            part = jnp.maximum(part, 0.0).astype(out.dtype)
            if n:
                res_out[q, n - 1] = part
                to_columns(q, n).start()
            else:
                out[pl.ds(pl.multiple_of((me * CHUNKS + q) * rows, rows), rows), :] = part

    for q in range(CHUNKS + 1):
        if q < CHUNKS:
            adj_load(q).wait()
            for k in (2, 1, 3):
                aggregate(q, k, agg_out.at[q, k - 1])
                to_rows(q, k).start()
            aggregate(q, 0, agg_in.at[q, 0])
        if q == 1:
            for load in w_loads:
                load.wait()
        if q:
            multiply(q - 1)
    for q in range(CHUNKS):
        for k in range(1, n_mp):
            to_rows(q, k).wait_send()
            to_columns(q, k).wait()


def layer(src_no, counts, own, partner, pulled, adj, unread, wts, bias):
    n_mp = wts.shape[0]
    tb, kb = adj.shape[:2]
    adj = adj.reshape(n_mp, CHUNKS, tb // n_mp // CHUNKS, kb, BLK, BLK)
    width = own.shape[-1]
    n_src = own.shape[0] + partner.shape[0] + pulled.shape[0]
    rows = tb // n_mp // CHUNKS * BLK
    any_spec = pl.BlockSpec(memory_space=pl.ANY)
    vmem_spec = pl.BlockSpec(memory_space=pltpu.VMEM)

    def kernel(*refs):
        layer_kernel(n_mp, *refs)

    return pl.pallas_call(
        kernel,
        out_shape=jax.ShapeDtypeStruct((tb * BLK, width), jnp.bfloat16),
        in_specs=[pl.BlockSpec(memory_space=pltpu.SMEM)] * 2 + [any_spec] * 6 + [vmem_spec],
        out_specs=vmem_spec,
        scratch_shapes=[
            pltpu.VMEM((n_src + 1, BLK, width), jnp.bfloat16),
            pltpu.VMEM(adj.shape, jnp.bfloat16),
            pltpu.VMEM((n_mp, n_mp, width, width), jnp.bfloat16),
            pltpu.VMEM((n_mp,) + bias.shape, jnp.float32),
            pltpu.VMEM((CHUNKS, n_mp - 1, rows, width), jnp.bfloat16),
            pltpu.VMEM((CHUNKS, n_mp, rows, width), jnp.bfloat16),
            pltpu.VMEM((CHUNKS, n_mp - 1, rows, width), jnp.bfloat16),
            pltpu.SemaphoreType.DMA((3 + CHUNKS,)),
            pltpu.SemaphoreType.DMA((n_mp, n_mp)),
            pltpu.SemaphoreType.DMA((n_mp - 1,)),
            pltpu.SemaphoreType.DMA((n_mp - 1,)),
        ]
        + [pltpu.SemaphoreType.DMA((CHUNKS, n_mp - 1))] * 4,
        compiler_params=pltpu.CompilerParams(
            collective_id=0, has_side_effects=True, vmem_limit_bytes=60 << 20
        ),
        name="layer",
    )(src_no, counts, own, partner, pulled, adj, unread, wts, bias)


def spread_kernel(
    hist, feat, asks, weight, hist_z, feat_y, asked, wts,
    hist_v, feat_v, weight_v, in_sem, own_sem,
    z_send, z_recv, y_send, y_recv, ask_send, ask_recv, w_send, w_recv,
):
    y, z, core, mp = (lax.axis_index(name) for name in ("y", "z", "core", "mp"))
    n_mp = wts.shape[0]
    z_piece = hist.shape[0] // Z_PIECES
    n_peers = NY * NC - 1

    def peer(n):
        at = n + 1
        return (y + at // NC) % NY, (core + at % NC) % NC

    loads = [
        pltpu.make_async_copy(hist, hist_v, in_sem.at[0]),
        pltpu.make_async_copy(feat, feat_v, in_sem.at[1]),
        pltpu.make_async_copy(weight, weight_v, in_sem.at[2]),
    ]
    own = [
        pltpu.make_async_copy(hist_v, hist_z.at[z], own_sem.at[0]),
        pltpu.make_async_copy(feat_v, feat_y.at[y], own_sem.at[1]),
        pltpu.make_async_copy(weight_v, wts.at[0], own_sem.at[2]),
        pltpu.make_async_copy(asks, asked.at[y * NC + core], own_sem.at[3]),
    ]
    for load in loads:
        load.start()

    barrier = pltpu.get_barrier_semaphore()
    for n in range(n_peers):
        to_y, to_core = peer(n)
        pl.semaphore_signal(
            barrier, inc=1, device_id={"y": to_y, "core": to_core}, device_id_type=MESH
        )
    for dz in (1, NZ - 1):
        pl.semaphore_signal(barrier, inc=1, device_id={"z": (z + dz) % NZ}, device_id_type=MESH)
    for k in range(1, n_mp):
        pl.semaphore_signal(barrier, inc=1, device_id={"mp": (mp + k) % n_mp}, device_id_type=MESH)
    pl.semaphore_wait(barrier, n_peers + 2 + n_mp - 1)

    def z_hop(up, s, p):
        at = (z + (1 - s if up else s - 1)) % NZ
        part = pl.ds(p * z_piece, z_piece)
        return pltpu.make_async_remote_copy(
            src_ref=(hist if s == 1 else hist_z.at[at]).at[part],
            dst_ref=hist_z.at[at, part],
            send_sem=z_send.at[0 if up else 1, s - 1, p],
            recv_sem=z_recv.at[0 if up else 1, s - 1, p],
            device_id={"z": (z + (1 if up else NZ - 1)) % NZ},
            device_id_type=MESH,
        )

    def y_hop(up, s, p):
        at = (y + (1 - s if up else s - 1)) % NY
        return pltpu.make_async_remote_copy(
            src_ref=(feat if s == 1 else feat_y.at[at]).at[p],
            dst_ref=feat_y.at[at, p],
            send_sem=y_send.at[0 if up else 1, s - 1, p],
            recv_sem=y_recv.at[0 if up else 1, s - 1, p],
            device_id={"y": (y + (1 if up else NY - 1)) % NY},
            device_id_type=MESH,
        )

    def order(size, pieces, up):
        last = range(pieces // 2) if up else range(pieces // 2, pieces)
        return [(up, s, p) for s in range(1, size // 2) for p in range(pieces)] + [
            (up, size // 2, p) for p in last
        ]

    def ask(n):
        to_y, to_core = peer(n)
        return pltpu.make_async_remote_copy(
            src_ref=asks,
            dst_ref=asked.at[y * NC + core],
            send_sem=ask_send.at[n],
            recv_sem=ask_recv.at[n],
            device_id={"y": to_y, "core": to_core},
            device_id_type=MESH,
        )

    def share(k):
        return pltpu.make_async_remote_copy(
            src_ref=weight,
            dst_ref=wts.at[k],
            send_sem=w_send.at[k - 1],
            recv_sem=w_recv.at[k - 1],
            device_id={"mp": (mp + k) % n_mp},
            device_id_type=MESH,
        )

    z_ways = [order(NZ, Z_PIECES, up) for up in (True, False)]
    y_ways = [order(NY, Y_PIECES, up) for up in (True, False)]
    for way in z_ways:
        for hop in way[:Z_AHEAD]:
            z_hop(*hop).start()
    for way in y_ways:
        for hop in way[:Y_PIECES]:
            y_hop(*hop).start()
    for n in range(n_peers):
        ask(n).start()
    for k in range(1, n_mp):
        share(k).start()
    for load in loads:
        load.wait()
    for copy in own:
        copy.start()

    for i in range(Z_AHEAD, len(z_ways[0])):
        for way in z_ways:
            up, s, p = way[i]
            z_hop(*way[i - Z_AHEAD]).wait_send()
            if s > 1:
                z_hop(up, s - 1, p).wait_recv()
            z_hop(up, s, p).start()
        if i == len(z_ways[0]) * 3 // 4:
            for way in y_ways:
                for up, s, p in way[Y_PIECES:]:
                    y_hop(up, s - 1, p).wait_recv()
                    y_hop(up, s, p).start()
    for make, ways, ahead in ((z_hop, z_ways, Z_AHEAD), (y_hop, y_ways, len(y_ways[0]))):
        for way in ways:
            for up, s, p in way:
                if (up, s + 1, p) not in way:
                    make(up, s, p).wait_recv()
            for hop in way[-ahead:]:
                make(*hop).wait_send()
    for n in range(n_peers):
        ask(n).wait()
    for k in range(1, n_mp):
        share(k).wait()
    for copy in own:
        copy.wait()


def spread(history, features, asks, weight, n_mp):
    any_spec = pl.BlockSpec(memory_space=pl.ANY)
    n_peers = NY * NC - 1

    def out(lead, value):
        return jax.ShapeDtypeStruct((lead,) + value.shape, value.dtype)

    return pl.pallas_call(
        spread_kernel,
        out_shape=(out(NZ, history), out(NY, features), out(NY * NC, asks), out(n_mp, weight)),
        in_specs=[any_spec] * 4,
        out_specs=(any_spec,) * 4,
        scratch_shapes=[
            pltpu.VMEM(history.shape, history.dtype),
            pltpu.VMEM(features.shape, features.dtype),
            pltpu.VMEM(weight.shape, weight.dtype),
            pltpu.SemaphoreType.DMA((3,)),
            pltpu.SemaphoreType.DMA((4,)),
            pltpu.SemaphoreType.DMA((2, NZ // 2, Z_PIECES)),
            pltpu.SemaphoreType.DMA((2, NZ // 2, Z_PIECES)),
            pltpu.SemaphoreType.DMA((2, NY // 2, Y_PIECES)),
            pltpu.SemaphoreType.DMA((2, NY // 2, Y_PIECES)),
            pltpu.SemaphoreType.DMA((n_peers,)),
            pltpu.SemaphoreType.DMA((n_peers,)),
            pltpu.SemaphoreType.DMA((n_mp - 1,)),
            pltpu.SemaphoreType.DMA((n_mp - 1,)),
        ],
        compiler_params=pltpu.CompilerParams(
            collective_id=2, has_side_effects=True, vmem_limit_bytes=60 << 20
        ),
        name="spread",
    )(history, features, asks, weight)


def pull_kernel(block_ids, hist, out, *scratch):
    shards = scratch[:NZ]
    picked, load_sem, keep_sem, send_sems, recv_sems = scratch[NZ:]
    y, core = lax.axis_index("y"), lax.axis_index("core")
    cap = picked.shape[2]
    me = y * NC + core
    n_peers = NY * NC - 1
    per_ask = NY * NZ * NC * cap

    def peer(n):
        at = 3 * (n + 1) % (NC * NY)
        return (y + at // NC) % NY, (core + at % NC) % NC

    loads = [pltpu.make_async_copy(hist.at[r], shards[r], load_sem.at[r]) for r in range(NZ)]
    for load in loads:
        load.start()
    barrier = pltpu.get_barrier_semaphore()
    for n in range(n_peers):
        to_y, to_core = peer(n)
        pl.semaphore_signal(
            barrier, inc=1, device_id={"y": to_y, "core": to_core}, device_id_type=MESH
        )
    pl.semaphore_wait(barrier, n_peers)

    def rows(r):
        return out.at[pl.ds((me * NZ + r) * cap, cap)]

    def give(r, n):
        to_y, to_core = peer(n)
        return pltpu.make_async_remote_copy(
            src_ref=picked.at[r, n],
            dst_ref=rows(r),
            send_sem=send_sems.at[r, n],
            recv_sem=recv_sems.at[r, n],
            device_id={"y": to_y, "core": to_core},
            device_id_type=MESH,
        )

    def keep(r):
        return pltpu.make_async_copy(picked.at[r, n_peers], rows(r), keep_sem.at[r])

    for r in range(NZ):
        loads[r].wait()

        def one(n, carry):
            to_y, to_core = peer(n)
            first = (to_y * NC + to_core) * per_ask + ((y * NZ + r) * NC + core) * cap
            for slot in range(cap):
                picked[r, n, slot] = shards[r][block_ids[first + slot]]

            @pl.when(n < n_peers)
            def _():
                give(r, n).start()

            return carry

        lax.fori_loop(0, n_peers + 1, one, 0)
        keep(r).start()

    def finish(r, carry):
        def one(n, inner):
            give(r, n).wait()
            return inner

        lax.fori_loop(0, n_peers, one, 0)
        keep(r).wait()
        return carry

    lax.fori_loop(0, NZ, finish, 0)


def pull(block_ids, hist):
    n_peers = NY * NC
    total = block_ids.shape[0] // n_peers
    cap = total // n_peers // NZ
    width = hist.shape[-1]
    any_spec = pl.BlockSpec(memory_space=pl.ANY)
    return pl.pallas_call(
        pull_kernel,
        out_shape=jax.ShapeDtypeStruct((total, BLK, width), jnp.bfloat16),
        in_specs=[pl.BlockSpec(memory_space=pltpu.SMEM), any_spec],
        out_specs=any_spec,
        scratch_shapes=[pltpu.VMEM(hist.shape[1:], jnp.bfloat16)] * NZ
        + [
            pltpu.VMEM((NZ, n_peers, cap, BLK, width), jnp.bfloat16),
            pltpu.SemaphoreType.DMA((NZ,)),
            pltpu.SemaphoreType.DMA((NZ,)),
            pltpu.SemaphoreType.DMA((NZ, n_peers - 1)),
            pltpu.SemaphoreType.DMA((NZ, n_peers - 1)),
        ],
        compiler_params=pltpu.CompilerParams(
            collective_id=1, has_side_effects=True, vmem_limit_bytes=60 << 20
        ),
        cost_estimate=pl.CostEstimate(flops=0, bytes_accessed=256 << 20, transcendentals=0),
        name="pull",
    )(block_ids, hist)


def per_device(
    features, history, adj_values, adj_sources, pull_list, pull_count, partner_mask, weight, bias
):
    row_count, width = features.shape
    row_blocks = row_count // BLK
    hist_blocks = history.shape[0] // BLK
    mask = partner_mask[0]
    n_mp = lax.axis_size("mp")
    y_mask = mask >> 4
    zc_mask = mask & (NZ * NC - 1)

    hist_z, feat_y, asked, wts = spread(
        history.reshape(hist_blocks, BLK, width),
        features.reshape(Y_PIECES, row_count // Y_PIECES, width),
        pull_list.reshape(1, -1),
        weight,
        n_mp,
    )

    half_way = lax.dynamic_index_in_dim(feat_y, lax.axis_index("y") ^ y_mask, keepdims=False)

    def pull_beside(m):
        def branch(rows, ids, hist):
            if m:
                rows = lax.ppermute(rows, ("z", "core"), [(s, s ^ m) for s in range(NZ * NC)])
            return rows, pull(ids, hist)

        return branch

    partner_rows, pulled = lax.switch(
        zc_mask,
        [pull_beside(m) for m in range(NZ * NC)],
        half_way,
        asked.reshape(-1),
        hist_z,
    )

    return layer(
        adj_sources.reshape(-1),
        pull_count.reshape(-1),
        features.reshape(row_blocks, BLK, width),
        partner_rows.reshape(row_blocks, BLK, width),
        pulled,
        adj_values,
        half_way,
        wts,
        bias.reshape(1, width),
    )


def solution(mesh):
    n_mp = mesh.devices.shape[1]
    fine = Mesh(mesh.devices.reshape(NY, NZ, NC, n_mp), ("y", "z", "core", "mp"))
    in_specs = (
        P(DP, "mp"),
        P(DP, "mp"),
        P(DP, None, None, None),
        P(DP, None),
        P(DP, None, None),
        P(DP, None),
        P(),
        P("mp", None),
        P("mp"),
    )
    return jax.shard_map(
        per_device, mesh=fine, in_specs=in_specs, out_specs=P(DP, "mp"), check_vma=False
    )
```

```python
import jax
import jax.numpy as jnp
from jax import lax
from jax.experimental import pallas as pl
from jax.experimental.pallas import tpu as pltpu
from jax.sharding import Mesh, PartitionSpec as P

NY, NZ, NC = 4, 8, 2
BLK = 128
CHUNKS = 4
Z_PIECES = 4
Z_AHEAD = 2
Y_PIECES = 4
DP = ("y", "z", "core")
MESH = pl.DeviceIdType.MESH


def layer_kernel(
    n_mp, src_idx, own, partner, pulled, adj, unread, w_rows, my_bias,
    out, srcs, tiles, wts, bias, agg_out, agg_in, res_out,
    load_sem, w_sem, bias_send, bias_recv, send_a, recv_a, send_b, recv_b,
):
    me = lax.axis_index("mp")
    per_chunk, kb = adj.shape[2:4]
    nb, n_pulled = own.shape[0], pulled.shape[0]
    n_src = 2 * nb + n_pulled
    rows = per_chunk * BLK

    def adj_load(q):
        return pltpu.make_async_copy(adj.at[:, q], tiles.at[:, q], load_sem.at[3 + q])

    loads = [
        pltpu.make_async_copy(own, srcs.at[pl.ds(0, nb)], load_sem.at[0]),
        pltpu.make_async_copy(partner, srcs.at[pl.ds(nb, nb)], load_sem.at[1]),
        pltpu.make_async_copy(pulled, srcs.at[pl.ds(2 * nb, n_pulled)], load_sem.at[2]),
    ]
    for load in loads:
        load.start()
    adj_load(0).start()
    srcs[n_src] = jnp.zeros(srcs.shape[1:], srcs.dtype)

    barrier = pltpu.get_barrier_semaphore()
    for k in range(1, n_mp):
        pl.semaphore_signal(barrier, inc=1, device_id={"mp": (me + k) % n_mp}, device_id_type=MESH)
    pl.semaphore_wait(barrier, n_mp - 1)

    def to_bias(k):
        return pltpu.make_async_remote_copy(
            src_ref=my_bias,
            dst_ref=bias.at[k],
            send_sem=bias_send.at[k - 1],
            recv_sem=bias_recv.at[k - 1],
            device_id={"mp": (me + k) % n_mp},
            device_id_type=MESH,
        )

    for k in range(1, n_mp):
        to_bias(k).start()
    bias[0] = my_bias[...]
    for load in loads:
        load.wait()
    adj_load(0).wait()
    for q in range(1, CHUNKS):
        adj_load(q).start()
    cols = own.shape[-1]
    w_loads = [
        pltpu.make_async_copy(
            w_rows.at[k, :, pl.ds(n * cols, cols)], wts.at[k, n], w_sem.at[k, n]
        )
        for k in range(n_mp)
        for n in range(n_mp)
    ]
    for load in w_loads:
        load.start()
    for k in range(1, n_mp):
        to_bias(k).wait()

    def to_rows(q, k):
        return pltpu.make_async_remote_copy(
            src_ref=agg_out.at[q, k - 1],
            dst_ref=agg_in.at[q, k],
            send_sem=send_a.at[q, k - 1],
            recv_sem=recv_a.at[q, k - 1],
            device_id={"mp": (me + k) % n_mp},
            device_id_type=MESH,
        )

    def to_columns(q, k):
        return pltpu.make_async_remote_copy(
            src_ref=res_out.at[q, k - 1],
            dst_ref=out.at[pl.ds(pl.multiple_of((me * CHUNKS + q) * rows, rows), rows)],
            send_sem=send_b.at[q, k - 1],
            recv_sem=recv_b.at[q, k - 1],
            device_id={"mp": (me + k) % n_mp},
            device_id_type=MESH,
        )

    def aggregate(q, k, dst):
        dev = (me + k) % n_mp

        def one(i, carry):
            t = (dev * CHUNKS + q) * per_chunk + i
            lhs = jnp.concatenate([tiles[dev, q, i, j] for j in range(kb)], axis=1)
            rhs = jnp.concatenate([srcs[src_idx[t, j]] for j in range(kb)], axis=0)
            block = jnp.dot(lhs, rhs, preferred_element_type=jnp.float32)
            dst[pl.ds(pl.multiple_of(i * BLK, BLK), BLK), :] = block.astype(dst.dtype)
            return carry

        lax.fori_loop(0, per_chunk, one, 0)

    def multiply(q):
        for k in range(1, n_mp):
            to_rows(q, k).wait_recv()
        for n in list(range(1, n_mp)) + [0]:
            part = bias[(n_mp - n) % n_mp] + jnp.zeros((rows, 1), jnp.float32)
            for k in range(n_mp):
                part = part + jnp.dot(
                    agg_in[q, k], wts[k, (me + n) % n_mp], preferred_element_type=jnp.float32
                )
            part = jnp.maximum(part, 0.0).astype(out.dtype)
            if n:
                res_out[q, n - 1] = part
                to_columns(q, n).start()
            else:
                out[pl.ds(pl.multiple_of((me * CHUNKS + q) * rows, rows), rows), :] = part

    for q in range(CHUNKS + 1):
        if q < CHUNKS:
            if q:
                adj_load(q).wait()
            for k in (2, 1, 3):
                aggregate(q, k, agg_out.at[q, k - 1])
                to_rows(q, k).start()
            aggregate(q, 0, agg_in.at[q, 0])
        if q == 1:
            for load in w_loads:
                load.wait()
        if q:
            multiply(q - 1)
    for q in range(CHUNKS):
        for k in range(1, n_mp):
            to_rows(q, k).wait_send()
            to_columns(q, k).wait()


def layer(src_idx, own, partner, pulled, adj, unread, wts, bias):
    n_mp = wts.shape[0]
    tb, kb = adj.shape[:2]
    adj = adj.reshape(n_mp, CHUNKS, tb // n_mp // CHUNKS, kb, BLK, BLK)
    width = own.shape[-1]
    n_src = own.shape[0] + partner.shape[0] + pulled.shape[0]
    rows = tb // n_mp // CHUNKS * BLK
    any_spec = pl.BlockSpec(memory_space=pl.ANY)
    vmem_spec = pl.BlockSpec(memory_space=pltpu.VMEM)

    def kernel(*refs):
        layer_kernel(n_mp, *refs)

    return pl.pallas_call(
        kernel,
        out_shape=jax.ShapeDtypeStruct((tb * BLK, width), jnp.bfloat16),
        in_specs=[pl.BlockSpec(memory_space=pltpu.SMEM)] + [any_spec] * 6 + [vmem_spec],
        out_specs=vmem_spec,
        scratch_shapes=[
            pltpu.VMEM((n_src + 1, BLK, width), jnp.bfloat16),
            pltpu.VMEM(adj.shape, jnp.bfloat16),
            pltpu.VMEM((n_mp, n_mp, width, width), jnp.bfloat16),
            pltpu.VMEM((n_mp,) + bias.shape, jnp.float32),
            pltpu.VMEM((CHUNKS, n_mp - 1, rows, width), jnp.bfloat16),
            pltpu.VMEM((CHUNKS, n_mp, rows, width), jnp.bfloat16),
            pltpu.VMEM((CHUNKS, n_mp - 1, rows, width), jnp.bfloat16),
            pltpu.SemaphoreType.DMA((3 + CHUNKS,)),
            pltpu.SemaphoreType.DMA((n_mp, n_mp)),
            pltpu.SemaphoreType.DMA((n_mp - 1,)),
            pltpu.SemaphoreType.DMA((n_mp - 1,)),
        ]
        + [pltpu.SemaphoreType.DMA((CHUNKS, n_mp - 1))] * 4,
        compiler_params=pltpu.CompilerParams(
            collective_id=0, has_side_effects=True, vmem_limit_bytes=50 << 20
        ),
        name="layer",
    )(src_idx, own, partner, pulled, adj, unread, wts, bias)


def spread_kernel(
    hist, feat, asks, weight, src_no, counts, hist_z, feat_y, asked, wts, src_idx,
    hist_v, feat_v, weight_v, in_sem, own_sem,
    z_send, z_recv, y_send, y_recv, ask_send, ask_recv, w_send, w_recv,
):
    y, z, core, mp = (lax.axis_index(name) for name in ("y", "z", "core", "mp"))
    n_mp = wts.shape[0]
    z_piece = hist.shape[0] // Z_PIECES
    n_peers = NY * NC - 1

    def peer(n):
        at = n + 1
        return (y + at // NC) % NY, (core + at % NC) % NC

    loads = [
        pltpu.make_async_copy(hist, hist_v, in_sem.at[0]),
        pltpu.make_async_copy(feat, feat_v, in_sem.at[1]),
        pltpu.make_async_copy(weight, weight_v, in_sem.at[2]),
    ]
    own = [
        pltpu.make_async_copy(hist_v, hist_z.at[z], own_sem.at[0]),
        pltpu.make_async_copy(feat_v, feat_y.at[y], own_sem.at[1]),
        pltpu.make_async_copy(weight_v, wts.at[0], own_sem.at[2]),
        pltpu.make_async_copy(asks, asked.at[y * NC + core], own_sem.at[3]),
    ]
    for load in loads:
        load.start()

    barrier = pltpu.get_barrier_semaphore()
    for n in range(n_peers):
        to_y, to_core = peer(n)
        pl.semaphore_signal(
            barrier, inc=1, device_id={"y": to_y, "core": to_core}, device_id_type=MESH
        )
    for dz in (1, NZ - 1):
        pl.semaphore_signal(barrier, inc=1, device_id={"z": (z + dz) % NZ}, device_id_type=MESH)
    for k in range(1, n_mp):
        pl.semaphore_signal(barrier, inc=1, device_id={"mp": (mp + k) % n_mp}, device_id_type=MESH)
    pl.semaphore_wait(barrier, n_peers + 2 + n_mp - 1)

    def z_hop(up, s, p):
        at = (z + (1 - s if up else s - 1)) % NZ
        part = pl.ds(p * z_piece, z_piece)
        return pltpu.make_async_remote_copy(
            src_ref=(hist if s == 1 else hist_z.at[at]).at[part],
            dst_ref=hist_z.at[at, part],
            send_sem=z_send.at[0 if up else 1, s - 1, p],
            recv_sem=z_recv.at[0 if up else 1, s - 1, p],
            device_id={"z": (z + (1 if up else NZ - 1)) % NZ},
            device_id_type=MESH,
        )

    def y_hop(up, s, p):
        at = (y + (1 - s if up else s - 1)) % NY
        return pltpu.make_async_remote_copy(
            src_ref=(feat if s == 1 else feat_y.at[at]).at[p],
            dst_ref=feat_y.at[at, p],
            send_sem=y_send.at[0 if up else 1, s - 1, p],
            recv_sem=y_recv.at[0 if up else 1, s - 1, p],
            device_id={"y": (y + (1 if up else NY - 1)) % NY},
            device_id_type=MESH,
        )

    def order(size, pieces, up):
        last = range(pieces // 2) if up else range(pieces // 2, pieces)
        return [(up, s, p) for s in range(1, size // 2) for p in range(pieces)] + [
            (up, size // 2, p) for p in last
        ]

    def ask(n):
        to_y, to_core = peer(n)
        return pltpu.make_async_remote_copy(
            src_ref=asks,
            dst_ref=asked.at[y * NC + core],
            send_sem=ask_send.at[n],
            recv_sem=ask_recv.at[n],
            device_id={"y": to_y, "core": to_core},
            device_id_type=MESH,
        )

    def share(k):
        return pltpu.make_async_remote_copy(
            src_ref=weight,
            dst_ref=wts.at[k],
            send_sem=w_send.at[k - 1],
            recv_sem=w_recv.at[k - 1],
            device_id={"mp": (mp + k) % n_mp},
            device_id_type=MESH,
        )

    own_blocks = feat.shape[0] * feat.shape[1] // BLK
    cap = asks.shape[-1] // counts.shape[0]

    def place(t, carry):
        for j in range(src_no.shape[1]):
            src = src_no[t, j]
            at = jnp.maximum(src - 2 * own_blocks, 0)
            owner, slot = at // cap, at % cap
            oy, oz, oc = owner // (NZ * NC), owner // NC % NZ, owner % NC
            moved = ((oy * NC + oc) * NZ + oz) * cap + slot
            moved = jnp.where(slot < counts[owner], moved, counts.shape[0] * cap)
            src_idx[t, j] = jnp.where(src < 2 * own_blocks, src, 2 * own_blocks + moved)
        return carry

    z_ways = [order(NZ, Z_PIECES, up) for up in (True, False)]
    y_ways = [order(NY, Y_PIECES, up) for up in (True, False)]
    for way in z_ways:
        for hop in way[:Z_AHEAD]:
            z_hop(*hop).start()
    for way in y_ways:
        for hop in way[:Y_PIECES]:
            y_hop(*hop).start()
    for n in range(n_peers):
        ask(n).start()
    for k in range(1, n_mp):
        share(k).start()
    for load in loads:
        load.wait()
    for copy in own:
        copy.start()

    for i in range(Z_AHEAD, len(z_ways[0])):
        for way in z_ways:
            up, s, p = way[i]
            z_hop(*way[i - Z_AHEAD]).wait_send()
            if s > 1:
                z_hop(up, s - 1, p).wait_recv()
            z_hop(up, s, p).start()
        some = -(-src_no.shape[0] // (len(z_ways[0]) - Z_AHEAD))
        first = (i - Z_AHEAD) * some
        lax.fori_loop(first, min(first + some, src_no.shape[0]), place, 0)
        if i == len(z_ways[0]) * 3 // 4:
            for way in y_ways:
                for up, s, p in way[Y_PIECES:]:
                    y_hop(up, s - 1, p).wait_recv()
                    y_hop(up, s, p).start()
    for make, ways, ahead in ((z_hop, z_ways, Z_AHEAD), (y_hop, y_ways, len(y_ways[0]))):
        for way in ways:
            for up, s, p in way:
                if (up, s + 1, p) not in way:
                    make(up, s, p).wait_recv()
            for hop in way[-ahead:]:
                make(*hop).wait_send()
    for n in range(n_peers):
        ask(n).wait()
    for k in range(1, n_mp):
        share(k).wait()
    for copy in own:
        copy.wait()


def spread(history, features, asks, weight, src_no, counts, n_mp):
    any_spec = pl.BlockSpec(memory_space=pl.ANY)
    smem_spec = pl.BlockSpec(memory_space=pltpu.SMEM)
    n_peers = NY * NC - 1

    def out(lead, value):
        return jax.ShapeDtypeStruct((lead,) + value.shape, value.dtype)

    return pl.pallas_call(
        spread_kernel,
        out_shape=(out(NZ, history), out(NY, features), out(NY * NC, asks), out(n_mp, weight),
                   jax.ShapeDtypeStruct(src_no.shape, jnp.int32)),
        in_specs=[any_spec] * 4 + [smem_spec] * 2,
        out_specs=(any_spec,) * 4 + (smem_spec,),
        scratch_shapes=[
            pltpu.VMEM(history.shape, history.dtype),
            pltpu.VMEM(features.shape, features.dtype),
            pltpu.VMEM(weight.shape, weight.dtype),
            pltpu.SemaphoreType.DMA((3,)),
            pltpu.SemaphoreType.DMA((4,)),
            pltpu.SemaphoreType.DMA((2, NZ // 2, Z_PIECES)),
            pltpu.SemaphoreType.DMA((2, NZ // 2, Z_PIECES)),
            pltpu.SemaphoreType.DMA((2, NY // 2, Y_PIECES)),
            pltpu.SemaphoreType.DMA((2, NY // 2, Y_PIECES)),
            pltpu.SemaphoreType.DMA((n_peers,)),
            pltpu.SemaphoreType.DMA((n_peers,)),
            pltpu.SemaphoreType.DMA((n_mp - 1,)),
            pltpu.SemaphoreType.DMA((n_mp - 1,)),
        ],
        compiler_params=pltpu.CompilerParams(
            collective_id=2, has_side_effects=True, vmem_limit_bytes=60 << 20
        ),
        name="spread",
    )(history, features, asks, weight, src_no, counts)


def pull_kernel(block_ids, hist, out, *scratch):
    shards = scratch[:NZ]
    picked, load_sem, keep_sem, send_sems, recv_sems = scratch[NZ:]
    y, core = lax.axis_index("y"), lax.axis_index("core")
    cap = picked.shape[2]
    me = y * NC + core
    n_peers = NY * NC - 1
    per_ask = NY * NZ * NC * cap

    def peer(n):
        at = 3 * (n + 1) % (NC * NY)
        return (y + at // NC) % NY, (core + at % NC) % NC

    loads = [pltpu.make_async_copy(hist.at[r], shards[r], load_sem.at[r]) for r in range(NZ)]
    for load in loads:
        load.start()
    barrier = pltpu.get_barrier_semaphore()
    for n in range(n_peers):
        to_y, to_core = peer(n)
        pl.semaphore_signal(
            barrier, inc=1, device_id={"y": to_y, "core": to_core}, device_id_type=MESH
        )
    pl.semaphore_wait(barrier, n_peers)

    def rows(r):
        return out.at[pl.ds((me * NZ + r) * cap, cap)]

    def give(r, n):
        to_y, to_core = peer(n)
        return pltpu.make_async_remote_copy(
            src_ref=picked.at[r, n],
            dst_ref=rows(r),
            send_sem=send_sems.at[r, n],
            recv_sem=recv_sems.at[r, n],
            device_id={"y": to_y, "core": to_core},
            device_id_type=MESH,
        )

    def keep(r):
        return pltpu.make_async_copy(picked.at[r, n_peers], rows(r), keep_sem.at[r])

    for r in range(NZ):
        loads[r].wait()

        def one(n, carry):
            to_y, to_core = peer(n)
            first = (to_y * NC + to_core) * per_ask + ((y * NZ + r) * NC + core) * cap
            for slot in range(cap):
                picked[r, n, slot] = shards[r][block_ids[first + slot]]

            @pl.when(n < n_peers)
            def _():
                give(r, n).start()

            return carry

        lax.fori_loop(0, n_peers + 1, one, 0)
        keep(r).start()

    def finish(r, carry):
        def one(n, inner):
            give(r, n).wait()
            return inner

        lax.fori_loop(0, n_peers, one, 0)
        keep(r).wait()
        return carry

    lax.fori_loop(0, NZ, finish, 0)


def pull(block_ids, hist):
    n_peers = NY * NC
    total = block_ids.shape[0] // n_peers
    cap = total // n_peers // NZ
    width = hist.shape[-1]
    any_spec = pl.BlockSpec(memory_space=pl.ANY)
    return pl.pallas_call(
        pull_kernel,
        out_shape=jax.ShapeDtypeStruct((total, BLK, width), jnp.bfloat16),
        in_specs=[pl.BlockSpec(memory_space=pltpu.SMEM), any_spec],
        out_specs=any_spec,
        scratch_shapes=[pltpu.VMEM(hist.shape[1:], jnp.bfloat16)] * NZ
        + [
            pltpu.VMEM((NZ, n_peers, cap, BLK, width), jnp.bfloat16),
            pltpu.SemaphoreType.DMA((NZ,)),
            pltpu.SemaphoreType.DMA((NZ,)),
            pltpu.SemaphoreType.DMA((NZ, n_peers - 1)),
            pltpu.SemaphoreType.DMA((NZ, n_peers - 1)),
        ],
        compiler_params=pltpu.CompilerParams(
            collective_id=1, has_side_effects=True, vmem_limit_bytes=60 << 20
        ),
        cost_estimate=pl.CostEstimate(flops=0, bytes_accessed=256 << 20, transcendentals=0),
        name="pull",
    )(block_ids, hist)


def per_device(
    features, history, adj_values, adj_sources, pull_list, pull_count, partner_mask, weight, bias
):
    row_count, width = features.shape
    row_blocks = row_count // BLK
    hist_blocks = history.shape[0] // BLK
    mask = partner_mask[0]
    n_mp = lax.axis_size("mp")
    y_mask = mask >> 4
    zc_mask = mask & (NZ * NC - 1)

    hist_z, feat_y, asked, wts, src_idx = spread(
        history.reshape(hist_blocks, BLK, width),
        features.reshape(Y_PIECES, row_count // Y_PIECES, width),
        pull_list.reshape(1, -1),
        weight,
        adj_sources,
        pull_count[0],
        n_mp,
    )

    half_way = lax.dynamic_index_in_dim(feat_y, lax.axis_index("y") ^ y_mask, keepdims=False)

    def pull_beside(m):
        def branch(rows, ids, hist):
            if m:
                rows = lax.ppermute(rows, ("z", "core"), [(s, s ^ m) for s in range(NZ * NC)])
            return rows, pull(ids, hist)

        return branch

    partner_rows, pulled = lax.switch(
        zc_mask,
        [pull_beside(m) for m in range(NZ * NC)],
        half_way,
        asked.reshape(-1),
        hist_z,
    )

    return layer(
        src_idx,
        features.reshape(row_blocks, BLK, width),
        partner_rows.reshape(row_blocks, BLK, width),
        pulled,
        adj_values,
        half_way,
        wts,
        bias.reshape(1, width),
    )


def solution(mesh):
    n_mp = mesh.devices.shape[1]
    fine = Mesh(mesh.devices.reshape(NY, NZ, NC, n_mp), ("y", "z", "core", "mp"))
    in_specs = (
        P(DP, "mp"),
        P(DP, "mp"),
        P(DP, None, None, None),
        P(DP, None),
        P(DP, None, None),
        P(DP, None),
        P(),
        P("mp", None),
        P("mp"),
    )
    return jax.shard_map(
        per_device, mesh=fine, in_specs=in_specs, out_specs=P(DP, "mp"), check_vma=False
    )
```

```python
import jax
import jax.numpy as jnp
from jax import lax
from jax.experimental import pallas as pl
from jax.experimental.pallas import tpu as pltpu
from jax.sharding import Mesh, PartitionSpec as P

NY, NZ, NC = 4, 8, 2
BLK = 128
CHUNKS = 4
Z_PIECES = 4
Z_AHEAD = 2
Y_PIECES = 4
DP = ("y", "z", "core")
MESH = pl.DeviceIdType.MESH


def layer_kernel(
    n_mp, src_idx, own, partner, near, pulled, adj, unread, w_rows, my_bias,
    out, srcs, tiles, wts, bias, agg_out, agg_in, res_out,
    load_sem, w_sem, bias_send, bias_recv, send_a, recv_a, send_b, recv_b,
):
    me = lax.axis_index("mp")
    per_chunk, kb = adj.shape[2:4]
    nb, n_near, n_pulled = own.shape[0], near.shape[0], pulled.shape[0]
    n_src = 2 * nb + n_near + n_pulled
    rows = per_chunk * BLK

    def adj_load(q):
        return pltpu.make_async_copy(adj.at[:, q], tiles.at[:, q], load_sem.at[4 + q])

    loads = [
        pltpu.make_async_copy(own, srcs.at[pl.ds(0, nb)], load_sem.at[0]),
        pltpu.make_async_copy(partner, srcs.at[pl.ds(nb, nb)], load_sem.at[1]),
        pltpu.make_async_copy(near, srcs.at[pl.ds(2 * nb, n_near)], load_sem.at[2]),
        pltpu.make_async_copy(pulled, srcs.at[pl.ds(2 * nb + n_near, n_pulled)], load_sem.at[3]),
    ]
    for load in loads:
        load.start()
    adj_load(0).start()
    srcs[n_src] = jnp.zeros(srcs.shape[1:], srcs.dtype)

    barrier = pltpu.get_barrier_semaphore()
    for k in range(1, n_mp):
        pl.semaphore_signal(barrier, inc=1, device_id={"mp": (me + k) % n_mp}, device_id_type=MESH)
    pl.semaphore_wait(barrier, n_mp - 1)

    def to_bias(k):
        return pltpu.make_async_remote_copy(
            src_ref=my_bias,
            dst_ref=bias.at[k],
            send_sem=bias_send.at[k - 1],
            recv_sem=bias_recv.at[k - 1],
            device_id={"mp": (me + k) % n_mp},
            device_id_type=MESH,
        )

    for k in range(1, n_mp):
        to_bias(k).start()
    bias[0] = my_bias[...]
    for load in loads:
        load.wait()
    adj_load(0).wait()
    for q in range(1, CHUNKS):
        adj_load(q).start()
    cols = own.shape[-1]
    w_loads = [
        pltpu.make_async_copy(
            w_rows.at[k, :, pl.ds(n * cols, cols)], wts.at[k, n], w_sem.at[k, n]
        )
        for k in range(n_mp)
        for n in range(n_mp)
    ]
    for load in w_loads:
        load.start()
    for k in range(1, n_mp):
        to_bias(k).wait()

    def to_rows(q, k):
        return pltpu.make_async_remote_copy(
            src_ref=agg_out.at[q, k - 1],
            dst_ref=agg_in.at[q, k],
            send_sem=send_a.at[q, k - 1],
            recv_sem=recv_a.at[q, k - 1],
            device_id={"mp": (me + k) % n_mp},
            device_id_type=MESH,
        )

    def to_columns(q, k):
        return pltpu.make_async_remote_copy(
            src_ref=res_out.at[q, k - 1],
            dst_ref=out.at[pl.ds(pl.multiple_of((me * CHUNKS + q) * rows, rows), rows)],
            send_sem=send_b.at[q, k - 1],
            recv_sem=recv_b.at[q, k - 1],
            device_id={"mp": (me + k) % n_mp},
            device_id_type=MESH,
        )

    def aggregate(q, k, dst):
        dev = (me + k) % n_mp

        def one(i, carry):
            t = (dev * CHUNKS + q) * per_chunk + i
            lhs = jnp.concatenate([tiles[dev, q, i, j] for j in range(kb)], axis=1)
            rhs = jnp.concatenate([srcs[src_idx[j, t]] for j in range(kb)], axis=0)
            block = jnp.dot(lhs, rhs, preferred_element_type=jnp.float32)
            dst[pl.ds(pl.multiple_of(i * BLK, BLK), BLK), :] = block.astype(dst.dtype)
            return carry

        lax.fori_loop(0, per_chunk, one, 0)

    def multiply(q):
        for k in range(1, n_mp):
            to_rows(q, k).wait_recv()
        for n in list(range(1, n_mp)) + [0]:
            part = bias[(n_mp - n) % n_mp] + jnp.zeros((rows, 1), jnp.float32)
            for k in range(n_mp):
                part = part + jnp.dot(
                    agg_in[q, k], wts[k, (me + n) % n_mp], preferred_element_type=jnp.float32
                )
            part = jnp.maximum(part, 0.0).astype(out.dtype)
            if n:
                res_out[q, n - 1] = part
                to_columns(q, n).start()
            else:
                out[pl.ds(pl.multiple_of((me * CHUNKS + q) * rows, rows), rows), :] = part

    for q in range(CHUNKS + 1):
        if q < CHUNKS:
            if q:
                adj_load(q).wait()
            for k in (2, 1, 3):
                aggregate(q, k, agg_out.at[q, k - 1])
                to_rows(q, k).start()
            aggregate(q, 0, agg_in.at[q, 0])
        if q == 1:
            for load in w_loads:
                load.wait()
        if q:
            multiply(q - 1)
    for q in range(CHUNKS):
        for k in range(1, n_mp):
            to_rows(q, k).wait_send()
            to_columns(q, k).wait()


def layer(src_idx, own, partner, near, pulled, adj, unread, wts, bias):
    n_mp = wts.shape[0]
    tb, kb = adj.shape[:2]
    adj = adj.reshape(n_mp, CHUNKS, tb // n_mp // CHUNKS, kb, BLK, BLK)
    width = own.shape[-1]
    n_src = own.shape[0] + partner.shape[0] + near.shape[0] + pulled.shape[0]
    rows = tb // n_mp // CHUNKS * BLK
    any_spec = pl.BlockSpec(memory_space=pl.ANY)
    vmem_spec = pl.BlockSpec(memory_space=pltpu.VMEM)

    def kernel(*refs):
        layer_kernel(n_mp, *refs)

    return pl.pallas_call(
        kernel,
        out_shape=jax.ShapeDtypeStruct((tb * BLK, width), jnp.bfloat16),
        in_specs=[pl.BlockSpec(memory_space=pltpu.SMEM)] + [any_spec] * 7 + [vmem_spec],
        out_specs=vmem_spec,
        scratch_shapes=[
            pltpu.VMEM((n_src + 1, BLK, width), jnp.bfloat16),
            pltpu.VMEM(adj.shape, jnp.bfloat16),
            pltpu.VMEM((n_mp, n_mp, width, width), jnp.bfloat16),
            pltpu.VMEM((n_mp,) + bias.shape, jnp.float32),
            pltpu.VMEM((CHUNKS, n_mp - 1, rows, width), jnp.bfloat16),
            pltpu.VMEM((CHUNKS, n_mp, rows, width), jnp.bfloat16),
            pltpu.VMEM((CHUNKS, n_mp - 1, rows, width), jnp.bfloat16),
            pltpu.SemaphoreType.DMA((4 + CHUNKS,)),
            pltpu.SemaphoreType.DMA((n_mp, n_mp)),
            pltpu.SemaphoreType.DMA((n_mp - 1,)),
            pltpu.SemaphoreType.DMA((n_mp - 1,)),
        ]
        + [pltpu.SemaphoreType.DMA((CHUNKS, n_mp - 1))] * 4,
        compiler_params=pltpu.CompilerParams(
            collective_id=0, has_side_effects=True, vmem_limit_bytes=50 << 20
        ),
        name="layer",
    )(src_idx, own, partner, near, pulled, adj, unread, wts, bias)


def spread_kernel(
    hist, feat, asks, weight, src_no, counts, hist_z, feat_y, asked, near, wts, src_idx,
    hist_v, feat_v, weight_v, asked_s, picked, in_sem, own_sem,
    z_send, z_recv, y_send, y_recv, ask_send, ask_recv, w_send, w_recv, near_send, near_recv,
):
    y, z, core, mp = (lax.axis_index(name) for name in ("y", "z", "core", "mp"))
    n_mp = wts.shape[0]
    z_piece = hist.shape[0] // Z_PIECES
    n_targets = src_no.shape[1]
    own_blocks = feat.shape[0] * feat.shape[1] // BLK
    cap = asks.shape[-1] // counts.shape[0]
    n_peers = NY * NC - 1

    def peer(n):
        at = (n + 1) % (NY * NC)
        return (y + at // NC) % NY, (core + at % NC) % NC

    loads = [
        pltpu.make_async_copy(hist, hist_v, in_sem.at[0]),
        pltpu.make_async_copy(feat, feat_v, in_sem.at[1]),
        pltpu.make_async_copy(weight, weight_v, in_sem.at[2]),
    ]
    own = [
        pltpu.make_async_copy(hist_v, hist_z.at[z], own_sem.at[0]),
        pltpu.make_async_copy(feat_v, feat_y.at[y], own_sem.at[1]),
        pltpu.make_async_copy(weight_v, wts.at[0], own_sem.at[2]),
        pltpu.make_async_copy(picked.at[n_peers], near.at[y * NC + core], own_sem.at[4]),
    ]
    own_ask = pltpu.make_async_copy(asks, asked.at[y * NC + core], own_sem.at[3])
    for load in loads:
        load.start()

    barrier = pltpu.get_barrier_semaphore()
    for n in range(n_peers):
        to_y, to_core = peer(n)
        pl.semaphore_signal(
            barrier, inc=1, device_id={"y": to_y, "core": to_core}, device_id_type=MESH
        )
    for dz in (1, NZ - 1):
        pl.semaphore_signal(barrier, inc=1, device_id={"z": (z + dz) % NZ}, device_id_type=MESH)
    for k in range(1, n_mp):
        pl.semaphore_signal(barrier, inc=1, device_id={"mp": (mp + k) % n_mp}, device_id_type=MESH)
    pl.semaphore_wait(barrier, n_peers + 2 + n_mp - 1)

    def z_hop(up, s, p):
        at = (z + (1 - s if up else s - 1)) % NZ
        part = pl.ds(p * z_piece, z_piece)
        return pltpu.make_async_remote_copy(
            src_ref=(hist if s == 1 else hist_z.at[at]).at[part],
            dst_ref=hist_z.at[at, part],
            send_sem=z_send.at[0 if up else 1, s - 1, p],
            recv_sem=z_recv.at[0 if up else 1, s - 1, p],
            device_id={"z": (z + (1 if up else NZ - 1)) % NZ},
            device_id_type=MESH,
        )

    def y_hop(up, s, p):
        at = (y + (1 - s if up else s - 1)) % NY
        return pltpu.make_async_remote_copy(
            src_ref=(feat if s == 1 else feat_y.at[at]).at[p],
            dst_ref=feat_y.at[at, p],
            send_sem=y_send.at[0 if up else 1, s - 1, p],
            recv_sem=y_recv.at[0 if up else 1, s - 1, p],
            device_id={"y": (y + (1 if up else NY - 1)) % NY},
            device_id_type=MESH,
        )

    def order(size, pieces, up):
        last = range(pieces // 2) if up else range(pieces // 2, pieces)
        return [(up, s, p) for s in range(1, size // 2) for p in range(pieces)] + [
            (up, size // 2, p) for p in last
        ]

    def ask(n):
        to_y, to_core = peer(n)
        return pltpu.make_async_remote_copy(
            src_ref=asks,
            dst_ref=asked.at[y * NC + core],
            send_sem=ask_send.at[n],
            recv_sem=ask_recv.at[n],
            device_id={"y": to_y, "core": to_core},
            device_id_type=MESH,
        )

    def share(k):
        return pltpu.make_async_remote_copy(
            src_ref=weight,
            dst_ref=wts.at[k],
            send_sem=w_send.at[k - 1],
            recv_sem=w_recv.at[k - 1],
            device_id={"mp": (mp + k) % n_mp},
            device_id_type=MESH,
        )

    def place(t, carry):
        for j in range(src_no.shape[0]):
            src = src_no[j, t]
            at = jnp.maximum(src - 2 * own_blocks, 0)
            owner, slot = at // cap, at % cap
            oy, oz, oc = owner // (NZ * NC), owner // NC % NZ, owner % NC
            moved = (((z + NZ - oz) % NZ * NY + oy) * NC + oc) * cap + slot
            moved = jnp.where(slot < counts[owner], moved, counts.shape[0] * cap)
            src_idx[j, t] = jnp.where(src < 2 * own_blocks, src, 2 * own_blocks + moved)
        return carry

    z_ways = [order(NZ, Z_PIECES, up) for up in (True, False)]
    y_ways = [order(NY, Y_PIECES, up) for up in (True, False)]
    for way in z_ways:
        for hop in way[:Z_AHEAD]:
            z_hop(*hop).start()
    for way in y_ways:
        for hop in way[:Y_PIECES]:
            y_hop(*hop).start()
    for n in range(n_peers):
        ask(n).start()
    for k in range(1, n_mp):
        share(k).start()
    own_ask.start()
    for load in loads:
        load.wait()

    own_ask.wait()
    for n in range(n_peers):
        ask(n).wait_recv()
    index = pltpu.make_async_copy(asked, asked_s, in_sem.at[3])
    index.start()
    index.wait()

    def near_give(n):
        to_y, to_core = peer(n)
        return pltpu.make_async_remote_copy(
            src_ref=picked.at[n],
            dst_ref=near.at[y * NC + core],
            send_sem=near_send.at[n],
            recv_sem=near_recv.at[n],
            device_id={"y": to_y, "core": to_core},
            device_id_type=MESH,
        )

    def serve(n, carry):
        to_y, to_core = peer(n)
        for slot in range(cap):
            at = ((y * NZ + z) * NC + core) * cap + slot
            picked[n, slot] = hist_v[asked_s[to_y * NC + to_core, 0, at]]

        @pl.when(n < n_peers)
        def _():
            near_give(n).start()

        return carry

    lax.fori_loop(0, n_peers + 1, serve, 0)
    for copy in own:
        copy.start()

    for i in range(Z_AHEAD, len(z_ways[0])):
        for way in z_ways:
            up, s, p = way[i]
            z_hop(*way[i - Z_AHEAD]).wait_send()
            if s > 1:
                z_hop(up, s - 1, p).wait_recv()
            z_hop(up, s, p).start()
        some = -(-n_targets // (len(z_ways[0]) - Z_AHEAD))
        first = (i - Z_AHEAD) * some
        lax.fori_loop(first, min(first + some, n_targets), place, 0)
        if i == len(z_ways[0]) * 3 // 4:
            for way in y_ways:
                for up, s, p in way[Y_PIECES:]:
                    y_hop(up, s - 1, p).wait_recv()
                    y_hop(up, s, p).start()
    for make, ways, ahead in ((z_hop, z_ways, Z_AHEAD), (y_hop, y_ways, len(y_ways[0]))):
        for way in ways:
            for up, s, p in way:
                if (up, s + 1, p) not in way:
                    make(up, s, p).wait_recv()
            for hop in way[-ahead:]:
                make(*hop).wait_send()
    for n in range(n_peers):
        ask(n).wait_send()
        near_give(n).wait()
    for k in range(1, n_mp):
        share(k).wait()
    for copy in own:
        copy.wait()


def spread(history, features, asks, weight, src_no, counts, n_mp):
    any_spec = pl.BlockSpec(memory_space=pl.ANY)
    smem_spec = pl.BlockSpec(memory_space=pltpu.SMEM)
    n_peers = NY * NC - 1

    def out(lead, value):
        return jax.ShapeDtypeStruct((lead,) + value.shape, value.dtype)

    cap = asks.shape[-1] // counts.shape[0]
    near = jax.ShapeDtypeStruct((NY * NC, cap) + history.shape[1:], history.dtype)

    return pl.pallas_call(
        spread_kernel,
        out_shape=(out(NZ, history), out(NY, features), out(NY * NC, asks), near, out(n_mp, weight),
                   jax.ShapeDtypeStruct(src_no.shape, jnp.int32)),
        in_specs=[any_spec] * 4 + [smem_spec] * 2,
        out_specs=(any_spec,) * 5 + (smem_spec,),
        scratch_shapes=[
            pltpu.VMEM(history.shape, history.dtype),
            pltpu.VMEM(features.shape, features.dtype),
            pltpu.VMEM(weight.shape, weight.dtype),
            pltpu.SMEM((NY * NC,) + asks.shape, asks.dtype),
            pltpu.VMEM(near.shape, near.dtype),
            pltpu.SemaphoreType.DMA((4,)),
            pltpu.SemaphoreType.DMA((5,)),
            pltpu.SemaphoreType.DMA((2, NZ // 2, Z_PIECES)),
            pltpu.SemaphoreType.DMA((2, NZ // 2, Z_PIECES)),
            pltpu.SemaphoreType.DMA((2, NY // 2, Y_PIECES)),
            pltpu.SemaphoreType.DMA((2, NY // 2, Y_PIECES)),
            pltpu.SemaphoreType.DMA((n_peers,)),
            pltpu.SemaphoreType.DMA((n_peers,)),
            pltpu.SemaphoreType.DMA((n_mp - 1,)),
            pltpu.SemaphoreType.DMA((n_mp - 1,)),
            pltpu.SemaphoreType.DMA((n_peers,)),
            pltpu.SemaphoreType.DMA((n_peers,)),
        ],
        compiler_params=pltpu.CompilerParams(
            collective_id=2, has_side_effects=True, vmem_limit_bytes=60 << 20
        ),
        name="spread",
    )(history, features, asks, weight, src_no, counts)


def pull_kernel(block_ids, hist, out, *scratch):
    shards = scratch[:NZ - 1]
    picked, load_sem, keep_sem, send_sems, recv_sems = scratch[NZ - 1:]
    y, z, core = lax.axis_index("y"), lax.axis_index("z"), lax.axis_index("core")
    cap = picked.shape[2]
    me = y * NC + core
    n_peers = NY * NC - 1
    per_ask = NY * NZ * NC * cap

    def peer(n):
        at = 3 * (n + 1) % (NC * NY)
        return (y + at // NC) % NY, (core + at % NC) % NC

    loads = [
        pltpu.make_async_copy(hist.at[(z + NZ - 1 - r) % NZ], shards[r], load_sem.at[r])
        for r in range(NZ - 1)
    ]
    for load in loads:
        load.start()
    barrier = pltpu.get_barrier_semaphore()
    for n in range(n_peers):
        to_y, to_core = peer(n)
        pl.semaphore_signal(
            barrier, inc=1, device_id={"y": to_y, "core": to_core}, device_id_type=MESH
        )
    pl.semaphore_wait(barrier, n_peers)

    def rows(r):
        return out.at[pl.ds((r * (n_peers + 1) + me) * cap, cap)]

    def give(r, n):
        to_y, to_core = peer(n)
        return pltpu.make_async_remote_copy(
            src_ref=picked.at[r, n],
            dst_ref=rows(r),
            send_sem=send_sems.at[r, n],
            recv_sem=recv_sems.at[r, n],
            device_id={"y": to_y, "core": to_core},
            device_id_type=MESH,
        )

    def keep(r):
        return pltpu.make_async_copy(picked.at[r, n_peers], rows(r), keep_sem.at[r])

    for r in range(NZ - 1):
        loads[r].wait()

        def one(n, carry):
            to_y, to_core = peer(n)
            first = (to_y * NC + to_core) * per_ask + ((y * NZ + (z + NZ - 1 - r) % NZ) * NC + core) * cap
            for slot in range(cap):
                picked[r, n, slot] = shards[r][block_ids[first + slot]]

            @pl.when(n < n_peers)
            def _():
                give(r, n).start()

            return carry

        lax.fori_loop(0, n_peers + 1, one, 0)
        keep(r).start()

    def finish(r, carry):
        def one(n, inner):
            give(r, n).wait()
            return inner

        lax.fori_loop(0, n_peers, one, 0)
        keep(r).wait()
        return carry

    lax.fori_loop(0, NZ - 1, finish, 0)


def pull(block_ids, hist):
    n_peers = NY * NC
    total = block_ids.shape[0] // n_peers
    cap = total // n_peers // NZ
    width = hist.shape[-1]
    any_spec = pl.BlockSpec(memory_space=pl.ANY)
    return pl.pallas_call(
        pull_kernel,
        out_shape=jax.ShapeDtypeStruct((total // NZ * (NZ - 1), BLK, width), jnp.bfloat16),
        in_specs=[pl.BlockSpec(memory_space=pltpu.SMEM), any_spec],
        out_specs=any_spec,
        scratch_shapes=[pltpu.VMEM(hist.shape[1:], jnp.bfloat16)] * (NZ - 1)
        + [
            pltpu.VMEM((NZ - 1, n_peers, cap, BLK, width), jnp.bfloat16),
            pltpu.SemaphoreType.DMA((NZ - 1,)),
            pltpu.SemaphoreType.DMA((NZ - 1,)),
            pltpu.SemaphoreType.DMA((NZ - 1, n_peers - 1)),
            pltpu.SemaphoreType.DMA((NZ - 1, n_peers - 1)),
        ],
        compiler_params=pltpu.CompilerParams(
            collective_id=1, has_side_effects=True, vmem_limit_bytes=60 << 20
        ),
        cost_estimate=pl.CostEstimate(flops=0, bytes_accessed=256 << 20, transcendentals=0),
        name="pull",
    )(block_ids, hist)


def per_device(
    features, history, adj_values, adj_sources, pull_list, pull_count, partner_mask, weight, bias
):
    row_count, width = features.shape
    row_blocks = row_count // BLK
    hist_blocks = history.shape[0] // BLK
    mask = partner_mask[0]
    n_mp = lax.axis_size("mp")
    y_mask = mask >> 4
    zc_mask = mask & (NZ * NC - 1)

    hist_z, feat_y, asked, near, wts, src_idx = spread(
        history.reshape(hist_blocks, BLK, width),
        features.reshape(Y_PIECES, row_count // Y_PIECES, width),
        pull_list.reshape(1, -1),
        weight,
        adj_sources.T,
        pull_count[0],
        n_mp,
    )

    half_way = lax.dynamic_index_in_dim(feat_y, lax.axis_index("y") ^ y_mask, keepdims=False)

    def pull_beside(m):
        def branch(rows, ids, hist):
            if m:
                rows = lax.ppermute(rows, ("z", "core"), [(s, s ^ m) for s in range(NZ * NC)])
            return rows, pull(ids, hist)

        return branch

    partner_rows, pulled = lax.switch(
        zc_mask,
        [pull_beside(m) for m in range(NZ * NC)],
        half_way,
        asked.reshape(-1),
        hist_z,
    )

    return layer(
        src_idx,
        features.reshape(row_blocks, BLK, width),
        partner_rows.reshape(row_blocks, BLK, width),
        near.reshape(-1, BLK, width),
        pulled,
        adj_values,
        half_way,
        wts,
        bias.reshape(1, width),
    )


def solution(mesh):
    n_mp = mesh.devices.shape[1]
    fine = Mesh(mesh.devices.reshape(NY, NZ, NC, n_mp), ("y", "z", "core", "mp"))
    in_specs = (
        P(DP, "mp"),
        P(DP, "mp"),
        P(DP, None, None, None),
        P(DP, None),
        P(DP, None, None),
        P(DP, None),
        P(),
        P("mp", None),
        P("mp"),
    )
    return jax.shard_map(
        per_device, mesh=fine, in_specs=in_specs, out_specs=P(DP, "mp"), check_vma=False
    )
```

```python
import jax
import jax.numpy as jnp
from jax import lax
from jax.experimental import pallas as pl
from jax.experimental.pallas import tpu as pltpu
from jax.sharding import Mesh, PartitionSpec as P

NY, NZ, NC = 4, 8, 2
BLK = 128
CHUNKS = 4
Z_PIECES = 4
Z_AHEAD = 2
Y_PIECES = 4
DP = ("y", "z", "core")
MESH = pl.DeviceIdType.MESH


def layer_kernel(
    n_mp, src_idx, own, partner, near, pulled, adj, unread, w_rows, my_bias,
    out, srcs, tiles, wts, bias, agg_out, agg_in, res_out,
    load_sem, w_sem, bias_send, bias_recv, send_a, recv_a, send_b, recv_b,
):
    me = lax.axis_index("mp")
    per_chunk, kb = adj.shape[2:4]
    nb, n_near, n_pulled = own.shape[0], near.shape[0], pulled.shape[0]
    n_src = 2 * nb + n_near + n_pulled
    rows = per_chunk * BLK

    def adj_load(q):
        return pltpu.make_async_copy(adj.at[:, q], tiles.at[:, q], load_sem.at[4 + q])

    loads = [
        pltpu.make_async_copy(own, srcs.at[pl.ds(0, nb)], load_sem.at[0]),
        pltpu.make_async_copy(partner, srcs.at[pl.ds(nb, nb)], load_sem.at[1]),
        pltpu.make_async_copy(near, srcs.at[pl.ds(2 * nb, n_near)], load_sem.at[2]),
        pltpu.make_async_copy(pulled, srcs.at[pl.ds(2 * nb + n_near, n_pulled)], load_sem.at[3]),
    ]
    for load in loads:
        load.start()
    adj_load(0).start()
    srcs[n_src] = jnp.zeros(srcs.shape[1:], srcs.dtype)

    barrier = pltpu.get_barrier_semaphore()
    for k in range(1, n_mp):
        pl.semaphore_signal(barrier, inc=1, device_id={"mp": (me + k) % n_mp}, device_id_type=MESH)
    pl.semaphore_wait(barrier, n_mp - 1)

    def to_bias(k):
        return pltpu.make_async_remote_copy(
            src_ref=my_bias,
            dst_ref=bias.at[k],
            send_sem=bias_send.at[k - 1],
            recv_sem=bias_recv.at[k - 1],
            device_id={"mp": (me + k) % n_mp},
            device_id_type=MESH,
        )

    for k in range(1, n_mp):
        to_bias(k).start()
    bias[0] = my_bias[...]
    for load in loads:
        load.wait()
    adj_load(0).wait()
    for q in range(1, CHUNKS):
        adj_load(q).start()
    cols = own.shape[-1]
    w_loads = [
        pltpu.make_async_copy(
            w_rows.at[k, :, pl.ds(n * cols, cols)], wts.at[k, n], w_sem.at[k, n]
        )
        for k in range(n_mp)
        for n in range(n_mp)
    ]
    for load in w_loads:
        load.start()
    for k in range(1, n_mp):
        to_bias(k).wait()

    def to_rows(q, k):
        return pltpu.make_async_remote_copy(
            src_ref=agg_out.at[q, k - 1],
            dst_ref=agg_in.at[q, k],
            send_sem=send_a.at[q, k - 1],
            recv_sem=recv_a.at[q, k - 1],
            device_id={"mp": (me + k) % n_mp},
            device_id_type=MESH,
        )

    def to_columns(q, k):
        return pltpu.make_async_remote_copy(
            src_ref=res_out.at[q, k - 1],
            dst_ref=out.at[pl.ds(pl.multiple_of((me * CHUNKS + q) * rows, rows), rows)],
            send_sem=send_b.at[q, k - 1],
            recv_sem=recv_b.at[q, k - 1],
            device_id={"mp": (me + k) % n_mp},
            device_id_type=MESH,
        )

    def aggregate(q, k, dst):
        dev = (me + k) % n_mp

        def one(i, carry):
            t = (dev * CHUNKS + q) * per_chunk + i
            lhs = jnp.concatenate([tiles[dev, q, i, j] for j in range(kb)], axis=1)
            rhs = jnp.concatenate([srcs[src_idx[j, t]] for j in range(kb)], axis=0)
            block = jnp.dot(lhs, rhs, preferred_element_type=jnp.float32)
            dst[pl.ds(pl.multiple_of(i * BLK, BLK), BLK), :] = block.astype(dst.dtype)
            return carry

        lax.fori_loop(0, per_chunk, one, 0)

    def multiply(q):
        for k in range(1, n_mp):
            to_rows(q, k).wait_recv()
        for n in list(range(1, n_mp)) + [0]:
            part = bias[(n_mp - n) % n_mp] + jnp.zeros((rows, 1), jnp.float32)
            for k in range(n_mp):
                part = part + jnp.dot(
                    agg_in[q, k], wts[k, (me + n) % n_mp], preferred_element_type=jnp.float32
                )
            part = jnp.maximum(part, 0.0).astype(out.dtype)
            if n:
                res_out[q, n - 1] = part
                to_columns(q, n).start()
            else:
                out[pl.ds(pl.multiple_of((me * CHUNKS + q) * rows, rows), rows), :] = part

    for q in range(CHUNKS + 1):
        if q < CHUNKS:
            if q:
                adj_load(q).wait()
            for k in (2, 1, 3):
                aggregate(q, k, agg_out.at[q, k - 1])
                to_rows(q, k).start()
            aggregate(q, 0, agg_in.at[q, 0])
        if q == 1:
            for load in w_loads:
                load.wait()
        if q:
            multiply(q - 1)
    for q in range(CHUNKS):
        for k in range(1, n_mp):
            to_rows(q, k).wait_send()
            to_columns(q, k).wait()


def layer(src_idx, own, partner, near, pulled, adj, unread, wts, bias):
    n_mp = wts.shape[0]
    tb, kb = adj.shape[:2]
    adj = adj.reshape(n_mp, CHUNKS, tb // n_mp // CHUNKS, kb, BLK, BLK)
    width = own.shape[-1]
    n_src = own.shape[0] + partner.shape[0] + near.shape[0] + pulled.shape[0]
    rows = tb // n_mp // CHUNKS * BLK
    any_spec = pl.BlockSpec(memory_space=pl.ANY)
    vmem_spec = pl.BlockSpec(memory_space=pltpu.VMEM)

    def kernel(*refs):
        layer_kernel(n_mp, *refs)

    return pl.pallas_call(
        kernel,
        out_shape=jax.ShapeDtypeStruct((tb * BLK, width), jnp.bfloat16),
        in_specs=[pl.BlockSpec(memory_space=pltpu.SMEM)] + [any_spec] * 7 + [vmem_spec],
        out_specs=vmem_spec,
        scratch_shapes=[
            pltpu.VMEM((n_src + 1, BLK, width), jnp.bfloat16),
            pltpu.VMEM(adj.shape, jnp.bfloat16),
            pltpu.VMEM((n_mp, n_mp, width, width), jnp.bfloat16),
            pltpu.VMEM((n_mp,) + bias.shape, jnp.float32),
            pltpu.VMEM((CHUNKS, n_mp - 1, rows, width), jnp.bfloat16),
            pltpu.VMEM((CHUNKS, n_mp, rows, width), jnp.bfloat16),
            pltpu.VMEM((CHUNKS, n_mp - 1, rows, width), jnp.bfloat16),
            pltpu.SemaphoreType.DMA((4 + CHUNKS,)),
            pltpu.SemaphoreType.DMA((n_mp, n_mp)),
            pltpu.SemaphoreType.DMA((n_mp - 1,)),
            pltpu.SemaphoreType.DMA((n_mp - 1,)),
        ]
        + [pltpu.SemaphoreType.DMA((CHUNKS, n_mp - 1))] * 4,
        compiler_params=pltpu.CompilerParams(
            collective_id=0, has_side_effects=True, vmem_limit_bytes=50 << 20
        ),
        name="layer",
    )(src_idx, own, partner, near, pulled, adj, unread, wts, bias)


def spread_kernel(
    hist, feat, asks, weight, src_no, counts, hist_z, feat_y, asked, near, wts, src_idx,
    hist_v, feat_v, weight_v, asked_s, picked, in_sem, own_sem,
    z_send, z_recv, y_send, y_recv, ask_send, ask_recv, w_send, w_recv, near_send, near_recv,
):
    y, z, core, mp = (lax.axis_index(name) for name in ("y", "z", "core", "mp"))
    n_mp = wts.shape[0]
    z_piece = hist.shape[0] // Z_PIECES
    n_targets = src_no.shape[1]
    own_blocks = feat.shape[0] * feat.shape[1] // BLK
    cap = asks.shape[-1] // counts.shape[0]
    n_peers = NY * NC - 1

    def peer(n):
        at = (n + 1) % (NY * NC)
        return (y + at // NC) % NY, (core + at % NC) % NC

    loads = [
        pltpu.make_async_copy(hist, hist_v, in_sem.at[0]),
        pltpu.make_async_copy(feat, feat_v, in_sem.at[1]),
        pltpu.make_async_copy(weight, weight_v, in_sem.at[2]),
    ]
    own = [
        pltpu.make_async_copy(hist_v, hist_z.at[z], own_sem.at[0]),
        pltpu.make_async_copy(feat_v, feat_y.at[y], own_sem.at[1]),
        pltpu.make_async_copy(weight_v, wts.at[0], own_sem.at[2]),
        pltpu.make_async_copy(picked.at[n_peers], near.at[y * NC + core], own_sem.at[4]),
    ]
    own_ask = pltpu.make_async_copy(asks, asked.at[y * NC + core], own_sem.at[3])
    for load in loads:
        load.start()

    barrier = pltpu.get_barrier_semaphore()
    for n in range(n_peers):
        to_y, to_core = peer(n)
        pl.semaphore_signal(
            barrier, inc=1, device_id={"y": to_y, "core": to_core}, device_id_type=MESH
        )
    for dz in (1, NZ - 1):
        pl.semaphore_signal(barrier, inc=1, device_id={"z": (z + dz) % NZ}, device_id_type=MESH)
    for k in range(1, n_mp):
        pl.semaphore_signal(barrier, inc=1, device_id={"mp": (mp + k) % n_mp}, device_id_type=MESH)
    pl.semaphore_wait(barrier, n_peers + 2 + n_mp - 1)

    def z_hop(up, s, p):
        at = (z + (1 - s if up else s - 1)) % NZ
        part = pl.ds(p * z_piece, z_piece)
        return pltpu.make_async_remote_copy(
            src_ref=(hist if s == 1 else hist_z.at[at]).at[part],
            dst_ref=hist_z.at[at, part],
            send_sem=z_send.at[0 if up else 1, s - 1, p],
            recv_sem=z_recv.at[0 if up else 1, s - 1, p],
            device_id={"z": (z + (1 if up else NZ - 1)) % NZ},
            device_id_type=MESH,
        )

    def y_hop(up, s, p):
        at = (y + (1 - s if up else s - 1)) % NY
        return pltpu.make_async_remote_copy(
            src_ref=(feat if s == 1 else feat_y.at[at]).at[p],
            dst_ref=feat_y.at[at, p],
            send_sem=y_send.at[0 if up else 1, s - 1, p],
            recv_sem=y_recv.at[0 if up else 1, s - 1, p],
            device_id={"y": (y + (1 if up else NY - 1)) % NY},
            device_id_type=MESH,
        )

    def order(size, pieces, up):
        last = range(pieces // 2) if up else range(pieces // 2, pieces)
        return [(up, s, p) for s in range(1, size // 2) for p in range(pieces)] + [
            (up, size // 2, p) for p in last
        ]

    def ask(n):
        to_y, to_core = peer(n)
        return pltpu.make_async_remote_copy(
            src_ref=asks,
            dst_ref=asked.at[y * NC + core],
            send_sem=ask_send.at[n],
            recv_sem=ask_recv.at[n],
            device_id={"y": to_y, "core": to_core},
            device_id_type=MESH,
        )

    def share(k):
        return pltpu.make_async_remote_copy(
            src_ref=weight,
            dst_ref=wts.at[k],
            send_sem=w_send.at[k - 1],
            recv_sem=w_recv.at[k - 1],
            device_id={"mp": (mp + k) % n_mp},
            device_id_type=MESH,
        )

    def place(t, carry):
        for j in range(src_no.shape[0]):
            src = src_no[j, t]
            at = jnp.maximum(src - 2 * own_blocks, 0)
            owner, slot = at // cap, at % cap
            oy, oz, oc = owner // (NZ * NC), owner // NC % NZ, owner % NC
            moved = (((z + NZ - oz) % NZ * NY + oy) * NC + oc) * cap + slot
            moved = jnp.where(slot < counts[owner], moved, counts.shape[0] * cap)
            src_idx[j, t] = jnp.where(src < 2 * own_blocks, src, 2 * own_blocks + moved)
        return carry

    z_ways = [order(NZ, Z_PIECES, up) for up in (True, False)]
    y_ways = [order(NY, Y_PIECES, up) for up in (True, False)]
    for n in range(n_peers):
        ask(n).start()
    own_ask.start()
    for way in z_ways:
        for hop in way[:Z_AHEAD]:
            z_hop(*hop).start()
    for load in loads:
        load.wait()

    own_ask.wait()
    for n in range(n_peers):
        ask(n).wait_recv()
    for way in y_ways:
        for hop in way[:Y_PIECES]:
            y_hop(*hop).start()
    for k in range(1, n_mp):
        share(k).start()
    index = pltpu.make_async_copy(asked, asked_s, in_sem.at[3])
    index.start()
    index.wait()

    def near_give(n):
        to_y, to_core = peer(n)
        return pltpu.make_async_remote_copy(
            src_ref=picked.at[n],
            dst_ref=near.at[y * NC + core],
            send_sem=near_send.at[n],
            recv_sem=near_recv.at[n],
            device_id={"y": to_y, "core": to_core},
            device_id_type=MESH,
        )

    def serve(n, carry):
        to_y, to_core = peer(n)
        for slot in range(cap):
            at = ((y * NZ + z) * NC + core) * cap + slot
            picked[n, slot] = hist_v[asked_s[to_y * NC + to_core, 0, at]]

        @pl.when(n < n_peers)
        def _():
            near_give(n).start()

        return carry

    lax.fori_loop(0, n_peers + 1, serve, 0)
    for copy in own:
        copy.start()

    for i in range(Z_AHEAD, len(z_ways[0])):
        for way in z_ways:
            up, s, p = way[i]
            z_hop(*way[i - Z_AHEAD]).wait_send()
            if s > 1:
                z_hop(up, s - 1, p).wait_recv()
            z_hop(up, s, p).start()
        some = -(-n_targets // (len(z_ways[0]) - Z_AHEAD))
        first = (i - Z_AHEAD) * some
        lax.fori_loop(first, min(first + some, n_targets), place, 0)
        if i == len(z_ways[0]) * 3 // 4:
            for way in y_ways:
                for up, s, p in way[Y_PIECES:]:
                    y_hop(up, s - 1, p).wait_recv()
                    y_hop(up, s, p).start()
    for make, ways, ahead in ((z_hop, z_ways, Z_AHEAD), (y_hop, y_ways, len(y_ways[0]))):
        for way in ways:
            for up, s, p in way:
                if (up, s + 1, p) not in way:
                    make(up, s, p).wait_recv()
            for hop in way[-ahead:]:
                make(*hop).wait_send()
    for n in range(n_peers):
        ask(n).wait_send()
        near_give(n).wait()
    for k in range(1, n_mp):
        share(k).wait()
    for copy in own:
        copy.wait()


def spread(history, features, asks, weight, src_no, counts, n_mp):
    any_spec = pl.BlockSpec(memory_space=pl.ANY)
    smem_spec = pl.BlockSpec(memory_space=pltpu.SMEM)
    n_peers = NY * NC - 1

    def out(lead, value):
        return jax.ShapeDtypeStruct((lead,) + value.shape, value.dtype)

    cap = asks.shape[-1] // counts.shape[0]
    near = jax.ShapeDtypeStruct((NY * NC, cap) + history.shape[1:], history.dtype)

    return pl.pallas_call(
        spread_kernel,
        out_shape=(out(NZ, history), out(NY, features), out(NY * NC, asks), near, out(n_mp, weight),
                   jax.ShapeDtypeStruct(src_no.shape, jnp.int32)),
        in_specs=[any_spec] * 4 + [smem_spec] * 2,
        out_specs=(any_spec,) * 5 + (smem_spec,),
        scratch_shapes=[
            pltpu.VMEM(history.shape, history.dtype),
            pltpu.VMEM(features.shape, features.dtype),
            pltpu.VMEM(weight.shape, weight.dtype),
            pltpu.SMEM((NY * NC,) + asks.shape, asks.dtype),
            pltpu.VMEM(near.shape, near.dtype),
            pltpu.SemaphoreType.DMA((4,)),
            pltpu.SemaphoreType.DMA((5,)),
            pltpu.SemaphoreType.DMA((2, NZ // 2, Z_PIECES)),
            pltpu.SemaphoreType.DMA((2, NZ // 2, Z_PIECES)),
            pltpu.SemaphoreType.DMA((2, NY // 2, Y_PIECES)),
            pltpu.SemaphoreType.DMA((2, NY // 2, Y_PIECES)),
            pltpu.SemaphoreType.DMA((n_peers,)),
            pltpu.SemaphoreType.DMA((n_peers,)),
            pltpu.SemaphoreType.DMA((n_mp - 1,)),
            pltpu.SemaphoreType.DMA((n_mp - 1,)),
            pltpu.SemaphoreType.DMA((n_peers,)),
            pltpu.SemaphoreType.DMA((n_peers,)),
        ],
        compiler_params=pltpu.CompilerParams(
            collective_id=2, has_side_effects=True, vmem_limit_bytes=60 << 20
        ),
        name="spread",
    )(history, features, asks, weight, src_no, counts)


def pull_kernel(block_ids, hist, out, *scratch):
    shards = scratch[:NZ - 1]
    picked, load_sem, keep_sem, send_sems, recv_sems = scratch[NZ - 1:]
    y, z, core = lax.axis_index("y"), lax.axis_index("z"), lax.axis_index("core")
    cap = picked.shape[2]
    me = y * NC + core
    n_peers = NY * NC - 1
    per_ask = NY * NZ * NC * cap

    def peer(n):
        at = 3 * (n + 1) % (NC * NY)
        return (y + at // NC) % NY, (core + at % NC) % NC

    loads = [
        pltpu.make_async_copy(hist.at[(z + NZ - 1 - r) % NZ], shards[r], load_sem.at[r])
        for r in range(NZ - 1)
    ]
    for load in loads:
        load.start()
    barrier = pltpu.get_barrier_semaphore()
    for n in range(n_peers):
        to_y, to_core = peer(n)
        pl.semaphore_signal(
            barrier, inc=1, device_id={"y": to_y, "core": to_core}, device_id_type=MESH
        )
    pl.semaphore_wait(barrier, n_peers)

    def rows(r):
        return out.at[pl.ds((r * (n_peers + 1) + me) * cap, cap)]

    def give(r, n):
        to_y, to_core = peer(n)
        return pltpu.make_async_remote_copy(
            src_ref=picked.at[r, n],
            dst_ref=rows(r),
            send_sem=send_sems.at[r, n],
            recv_sem=recv_sems.at[r, n],
            device_id={"y": to_y, "core": to_core},
            device_id_type=MESH,
        )

    def keep(r):
        return pltpu.make_async_copy(picked.at[r, n_peers], rows(r), keep_sem.at[r])

    for r in range(NZ - 1):
        loads[r].wait()

        def one(n, carry):
            to_y, to_core = peer(n)
            first = (to_y * NC + to_core) * per_ask + ((y * NZ + (z + NZ - 1 - r) % NZ) * NC + core) * cap
            for slot in range(cap):
                picked[r, n, slot] = shards[r][block_ids[first + slot]]

            @pl.when(n < n_peers)
            def _():
                give(r, n).start()

            return carry

        lax.fori_loop(0, n_peers + 1, one, 0)
        keep(r).start()

    def finish(r, carry):
        def one(n, inner):
            give(r, n).wait()
            return inner

        lax.fori_loop(0, n_peers, one, 0)
        keep(r).wait()
        return carry

    lax.fori_loop(0, NZ - 1, finish, 0)


def pull(block_ids, hist):
    n_peers = NY * NC
    total = block_ids.shape[0] // n_peers
    cap = total // n_peers // NZ
    width = hist.shape[-1]
    any_spec = pl.BlockSpec(memory_space=pl.ANY)
    return pl.pallas_call(
        pull_kernel,
        out_shape=jax.ShapeDtypeStruct((total // NZ * (NZ - 1), BLK, width), jnp.bfloat16),
        in_specs=[pl.BlockSpec(memory_space=pltpu.SMEM), any_spec],
        out_specs=any_spec,
        scratch_shapes=[pltpu.VMEM(hist.shape[1:], jnp.bfloat16)] * (NZ - 1)
        + [
            pltpu.VMEM((NZ - 1, n_peers, cap, BLK, width), jnp.bfloat16),
            pltpu.SemaphoreType.DMA((NZ - 1,)),
            pltpu.SemaphoreType.DMA((NZ - 1,)),
            pltpu.SemaphoreType.DMA((NZ - 1, n_peers - 1)),
            pltpu.SemaphoreType.DMA((NZ - 1, n_peers - 1)),
        ],
        compiler_params=pltpu.CompilerParams(
            collective_id=1, has_side_effects=True, vmem_limit_bytes=60 << 20
        ),
        cost_estimate=pl.CostEstimate(flops=0, bytes_accessed=256 << 20, transcendentals=0),
        name="pull",
    )(block_ids, hist)


def per_device(
    features, history, adj_values, adj_sources, pull_list, pull_count, partner_mask, weight, bias
):
    row_count, width = features.shape
    row_blocks = row_count // BLK
    hist_blocks = history.shape[0] // BLK
    mask = partner_mask[0]
    n_mp = lax.axis_size("mp")
    y_mask = mask >> 4
    zc_mask = mask & (NZ * NC - 1)

    hist_z, feat_y, asked, near, wts, src_idx = spread(
        history.reshape(hist_blocks, BLK, width),
        features.reshape(Y_PIECES, row_count // Y_PIECES, width),
        pull_list.reshape(1, -1),
        weight,
        adj_sources.T,
        pull_count[0],
        n_mp,
    )

    half_way = lax.dynamic_index_in_dim(feat_y, lax.axis_index("y") ^ y_mask, keepdims=False)

    def pull_beside(m):
        def branch(rows, ids, hist):
            if m:
                rows = lax.ppermute(rows, ("z", "core"), [(s, s ^ m) for s in range(NZ * NC)])
            return rows, pull(ids, hist)

        return branch

    partner_rows, pulled = lax.switch(
        zc_mask,
        [pull_beside(m) for m in range(NZ * NC)],
        half_way,
        asked.reshape(-1),
        hist_z,
    )

    return layer(
        src_idx,
        features.reshape(row_blocks, BLK, width),
        partner_rows.reshape(row_blocks, BLK, width),
        near.reshape(-1, BLK, width),
        pulled,
        adj_values,
        half_way,
        wts,
        bias.reshape(1, width),
    )


def solution(mesh):
    n_mp = mesh.devices.shape[1]
    fine = Mesh(mesh.devices.reshape(NY, NZ, NC, n_mp), ("y", "z", "core", "mp"))
    in_specs = (
        P(DP, "mp"),
        P(DP, "mp"),
        P(DP, None, None, None),
        P(DP, None),
        P(DP, None, None),
        P(DP, None),
        P(),
        P("mp", None),
        P("mp"),
    )
    return jax.shard_map(
        per_device, mesh=fine, in_specs=in_specs, out_specs=P(DP, "mp"), check_vma=False
    )
```

```python
import jax
import jax.numpy as jnp
from jax import lax
from jax.experimental import pallas as pl
from jax.experimental.pallas import tpu as pltpu
from jax.sharding import Mesh, PartitionSpec as P

NY, NZ, NC = 4, 8, 2
BLK = 128
CHUNKS = 4
LOADS = 4
Z_PIECES = 4
Z_AHEAD = 2
Y_PIECES = 4
DP = ("y", "z", "core")
MESH = pl.DeviceIdType.MESH


def layer_kernel(
    n_mp, src_idx, own, partner, near, pulled, adj, unread, w_rows, my_bias,
    out, srcs, tiles, wts, bias, agg_out, agg_in, res_out,
    load_sem, w_sem, bias_send, bias_recv, send_a, recv_a, send_b, recv_b,
):
    me = lax.axis_index("mp")
    per_chunk, kb = adj.shape[2:4]
    nb, n_near, n_pulled = own.shape[0], near.shape[0], pulled.shape[0]
    n_src = 2 * nb + n_near + n_pulled
    rows = per_chunk * BLK

    def adj_load(q):
        return pltpu.make_async_copy(adj.at[:, q], tiles.at[:, q], load_sem.at[3 + LOADS + q])

    loads = [
        pltpu.make_async_copy(own, srcs.at[pl.ds(0, nb)], load_sem.at[0]),
        pltpu.make_async_copy(partner, srcs.at[pl.ds(nb, nb)], load_sem.at[1]),
        pltpu.make_async_copy(near, srcs.at[pl.ds(2 * nb, n_near)], load_sem.at[2]),
    ]
    part = n_pulled // LOADS
    for i in range(LOADS):
        loads.append(
            pltpu.make_async_copy(
                pulled.at[pl.ds(i * part, part)],
                srcs.at[pl.ds(2 * nb + n_near + i * part, part)],
                load_sem.at[3 + i],
            )
        )
    for load in loads:
        load.start()
    adj_load(0).start()
    srcs[n_src] = jnp.zeros(srcs.shape[1:], srcs.dtype)

    barrier = pltpu.get_barrier_semaphore()
    for k in range(1, n_mp):
        pl.semaphore_signal(barrier, inc=1, device_id={"mp": (me + k) % n_mp}, device_id_type=MESH)
    pl.semaphore_wait(barrier, n_mp - 1)

    def to_bias(k):
        return pltpu.make_async_remote_copy(
            src_ref=my_bias,
            dst_ref=bias.at[k],
            send_sem=bias_send.at[k - 1],
            recv_sem=bias_recv.at[k - 1],
            device_id={"mp": (me + k) % n_mp},
            device_id_type=MESH,
        )

    for k in range(1, n_mp):
        to_bias(k).start()
    bias[0] = my_bias[...]
    for load in loads:
        load.wait()
    adj_load(0).wait()
    for q in range(1, CHUNKS):
        adj_load(q).start()
    cols = own.shape[-1]
    w_loads = [
        pltpu.make_async_copy(
            w_rows.at[k, :, pl.ds(n * cols, cols)], wts.at[k, n], w_sem.at[k, n]
        )
        for k in range(n_mp)
        for n in range(n_mp)
    ]
    for load in w_loads:
        load.start()
    for k in range(1, n_mp):
        to_bias(k).wait()

    def to_rows(q, k):
        return pltpu.make_async_remote_copy(
            src_ref=agg_out.at[q, k - 1],
            dst_ref=agg_in.at[q, k],
            send_sem=send_a.at[q, k - 1],
            recv_sem=recv_a.at[q, k - 1],
            device_id={"mp": (me + k) % n_mp},
            device_id_type=MESH,
        )

    def to_columns(q, k):
        return pltpu.make_async_remote_copy(
            src_ref=res_out.at[q, k - 1],
            dst_ref=out.at[pl.ds(pl.multiple_of((me * CHUNKS + q) * rows, rows), rows)],
            send_sem=send_b.at[q, k - 1],
            recv_sem=recv_b.at[q, k - 1],
            device_id={"mp": (me + k) % n_mp},
            device_id_type=MESH,
        )

    def aggregate(q, k, dst):
        dev = (me + k) % n_mp

        def one(i, carry):
            t = (dev * CHUNKS + q) * per_chunk + i
            lhs = jnp.concatenate([tiles[dev, q, i, j] for j in range(kb)], axis=1)
            rhs = jnp.concatenate([srcs[src_idx[j, t]] for j in range(kb)], axis=0)
            block = jnp.dot(lhs, rhs, preferred_element_type=jnp.float32)
            dst[pl.ds(pl.multiple_of(i * BLK, BLK), BLK), :] = block.astype(dst.dtype)
            return carry

        lax.fori_loop(0, per_chunk, one, 0)

    def multiply(q):
        for k in range(1, n_mp):
            to_rows(q, k).wait_recv()
        for n in list(range(1, n_mp)) + [0]:
            part = bias[(n_mp - n) % n_mp] + jnp.zeros((rows, 1), jnp.float32)
            for k in range(n_mp):
                part = part + jnp.dot(
                    agg_in[q, k], wts[k, (me + n) % n_mp], preferred_element_type=jnp.float32
                )
            part = jnp.maximum(part, 0.0).astype(out.dtype)
            if n:
                res_out[q, n - 1] = part
                to_columns(q, n).start()
            else:
                out[pl.ds(pl.multiple_of((me * CHUNKS + q) * rows, rows), rows), :] = part

    for q in range(CHUNKS + 1):
        if q < CHUNKS:
            if q:
                adj_load(q).wait()
            for k in (2, 1, 3):
                aggregate(q, k, agg_out.at[q, k - 1])
                to_rows(q, k).start()
            aggregate(q, 0, agg_in.at[q, 0])
        if q == 1:
            for load in w_loads:
                load.wait()
        if q:
            multiply(q - 1)
    for q in range(CHUNKS):
        for k in range(1, n_mp):
            to_rows(q, k).wait_send()
            to_columns(q, k).wait()


def layer(src_idx, own, partner, near, pulled, adj, unread, wts, bias):
    n_mp = wts.shape[0]
    tb, kb = adj.shape[:2]
    adj = adj.reshape(n_mp, CHUNKS, tb // n_mp // CHUNKS, kb, BLK, BLK)
    width = own.shape[-1]
    n_src = own.shape[0] + partner.shape[0] + near.shape[0] + pulled.shape[0]
    rows = tb // n_mp // CHUNKS * BLK
    any_spec = pl.BlockSpec(memory_space=pl.ANY)
    vmem_spec = pl.BlockSpec(memory_space=pltpu.VMEM)

    def kernel(*refs):
        layer_kernel(n_mp, *refs)

    return pl.pallas_call(
        kernel,
        out_shape=jax.ShapeDtypeStruct((tb * BLK, width), jnp.bfloat16),
        in_specs=[pl.BlockSpec(memory_space=pltpu.SMEM)] + [any_spec] * 7 + [vmem_spec],
        out_specs=vmem_spec,
        scratch_shapes=[
            pltpu.VMEM((n_src + 1, BLK, width), jnp.bfloat16),
            pltpu.VMEM(adj.shape, jnp.bfloat16),
            pltpu.VMEM((n_mp, n_mp, width, width), jnp.bfloat16),
            pltpu.VMEM((n_mp,) + bias.shape, jnp.float32),
            pltpu.VMEM((CHUNKS, n_mp - 1, rows, width), jnp.bfloat16),
            pltpu.VMEM((CHUNKS, n_mp, rows, width), jnp.bfloat16),
            pltpu.VMEM((CHUNKS, n_mp - 1, rows, width), jnp.bfloat16),
            pltpu.SemaphoreType.DMA((3 + LOADS + CHUNKS,)),
            pltpu.SemaphoreType.DMA((n_mp, n_mp)),
            pltpu.SemaphoreType.DMA((n_mp - 1,)),
            pltpu.SemaphoreType.DMA((n_mp - 1,)),
        ]
        + [pltpu.SemaphoreType.DMA((CHUNKS, n_mp - 1))] * 4,
        compiler_params=pltpu.CompilerParams(
            collective_id=0, has_side_effects=True, vmem_limit_bytes=50 << 20
        ),
        name="layer",
    )(src_idx, own, partner, near, pulled, adj, unread, wts, bias)


def spread_kernel(
    hist, feat, asks, weight, src_no, counts, hist_z, feat_y, asked, near, wts, src_idx,
    hist_v, feat_v, weight_v, asked_s, picked, in_sem, own_sem,
    z_send, z_recv, y_send, y_recv, ask_send, ask_recv, w_send, w_recv, near_send, near_recv,
):
    y, z, core, mp = (lax.axis_index(name) for name in ("y", "z", "core", "mp"))
    n_mp = wts.shape[0]
    z_piece = hist.shape[0] // Z_PIECES
    n_targets = src_no.shape[1]
    own_blocks = feat.shape[0] * feat.shape[1] // BLK
    cap = asks.shape[-1] // counts.shape[0]
    n_peers = NY * NC - 1

    def peer(n):
        at = (n + 1) % (NY * NC)
        return (y + at // NC) % NY, (core + at % NC) % NC

    loads = [
        pltpu.make_async_copy(hist, hist_v, in_sem.at[0]),
        pltpu.make_async_copy(feat, feat_v, in_sem.at[1]),
        pltpu.make_async_copy(weight, weight_v, in_sem.at[2]),
    ]
    own = [
        pltpu.make_async_copy(hist_v, hist_z.at[z], own_sem.at[0]),
        pltpu.make_async_copy(feat_v, feat_y.at[y], own_sem.at[1]),
        pltpu.make_async_copy(weight_v, wts.at[0], own_sem.at[2]),
        pltpu.make_async_copy(picked.at[n_peers], near.at[y * NC + core], own_sem.at[4]),
    ]
    own_ask = pltpu.make_async_copy(asks, asked.at[y * NC + core], own_sem.at[3])
    for load in loads:
        load.start()

    barrier = pltpu.get_barrier_semaphore()
    for n in range(n_peers):
        to_y, to_core = peer(n)
        pl.semaphore_signal(
            barrier, inc=1, device_id={"y": to_y, "core": to_core}, device_id_type=MESH
        )
    for dz in (1, NZ - 1):
        pl.semaphore_signal(barrier, inc=1, device_id={"z": (z + dz) % NZ}, device_id_type=MESH)
    for k in range(1, n_mp):
        pl.semaphore_signal(barrier, inc=1, device_id={"mp": (mp + k) % n_mp}, device_id_type=MESH)
    pl.semaphore_wait(barrier, n_peers + 2 + n_mp - 1)

    def z_hop(up, s, p):
        at = (z + (1 - s if up else s - 1)) % NZ
        part = pl.ds(p * z_piece, z_piece)
        return pltpu.make_async_remote_copy(
            src_ref=(hist if s == 1 else hist_z.at[at]).at[part],
            dst_ref=hist_z.at[at, part],
            send_sem=z_send.at[0 if up else 1, s - 1, p],
            recv_sem=z_recv.at[0 if up else 1, s - 1, p],
            device_id={"z": (z + (1 if up else NZ - 1)) % NZ},
            device_id_type=MESH,
        )

    def y_hop(up, s, p):
        at = (y + (1 - s if up else s - 1)) % NY
        return pltpu.make_async_remote_copy(
            src_ref=(feat if s == 1 else feat_y.at[at]).at[p],
            dst_ref=feat_y.at[at, p],
            send_sem=y_send.at[0 if up else 1, s - 1, p],
            recv_sem=y_recv.at[0 if up else 1, s - 1, p],
            device_id={"y": (y + (1 if up else NY - 1)) % NY},
            device_id_type=MESH,
        )

    def order(size, pieces, up):
        last = range(pieces // 2) if up else range(pieces // 2, pieces)
        return [(up, s, p) for s in range(1, size // 2) for p in range(pieces)] + [
            (up, size // 2, p) for p in last
        ]

    def ask(n):
        to_y, to_core = peer(n)
        return pltpu.make_async_remote_copy(
            src_ref=asks,
            dst_ref=asked.at[y * NC + core],
            send_sem=ask_send.at[n],
            recv_sem=ask_recv.at[n],
            device_id={"y": to_y, "core": to_core},
            device_id_type=MESH,
        )

    def share(k):
        return pltpu.make_async_remote_copy(
            src_ref=weight,
            dst_ref=wts.at[k],
            send_sem=w_send.at[k - 1],
            recv_sem=w_recv.at[k - 1],
            device_id={"mp": (mp + k) % n_mp},
            device_id_type=MESH,
        )

    def place(t, carry):
        for j in range(src_no.shape[0]):
            src = src_no[j, t]
            at = jnp.maximum(src - 2 * own_blocks, 0)
            owner, slot = at // cap, at % cap
            oy, oz, oc = owner // (NZ * NC), owner // NC % NZ, owner % NC
            moved = (((z + NZ - oz) % NZ * NY + oy) * NC + oc) * cap + slot
            moved = jnp.where(slot < counts[owner], moved, counts.shape[0] * cap)
            src_idx[j, t] = jnp.where(src < 2 * own_blocks, src, 2 * own_blocks + moved)
        return carry

    z_ways = [order(NZ, Z_PIECES, up) for up in (True, False)]
    y_ways = [order(NY, Y_PIECES, up) for up in (True, False)]
    for n in range(n_peers):
        ask(n).start()
    own_ask.start()
    for way in z_ways:
        for hop in way[:Z_AHEAD]:
            z_hop(*hop).start()
    for load in loads:
        load.wait()

    own_ask.wait()
    for n in range(n_peers):
        ask(n).wait_recv()
    for way in y_ways:
        for hop in way[:Y_PIECES]:
            y_hop(*hop).start()
    for k in range(1, n_mp):
        share(k).start()
    index = pltpu.make_async_copy(asked, asked_s, in_sem.at[3])
    index.start()
    index.wait()

    def near_give(n):
        to_y, to_core = peer(n)
        return pltpu.make_async_remote_copy(
            src_ref=picked.at[n],
            dst_ref=near.at[y * NC + core],
            send_sem=near_send.at[n],
            recv_sem=near_recv.at[n],
            device_id={"y": to_y, "core": to_core},
            device_id_type=MESH,
        )

    def serve(n, carry):
        to_y, to_core = peer(n)
        for slot in range(cap):
            at = ((y * NZ + z) * NC + core) * cap + slot
            picked[n, slot] = hist_v[asked_s[to_y * NC + to_core, 0, at]]

        @pl.when(n < n_peers)
        def _():
            near_give(n).start()

        return carry

    for copy in own[:-1]:
        copy.start()

    for i in range(Z_AHEAD, len(z_ways[0])):
        for way in z_ways:
            up, s, p = way[i]
            z_hop(*way[i - Z_AHEAD]).wait_send()
            if s > 1:
                z_hop(up, s - 1, p).wait_recv()
            z_hop(up, s, p).start()
        some = -(-n_targets // (len(z_ways[0]) - Z_AHEAD))
        first = (i - Z_AHEAD) * some
        lax.fori_loop(first, min(first + some, n_targets), place, 0)
        if i == len(z_ways[0]) * 3 // 4:
            for way in y_ways:
                for up, s, p in way[Y_PIECES:]:
                    y_hop(up, s - 1, p).wait_recv()
                    y_hop(up, s, p).start()
            lax.fori_loop(0, n_peers + 1, serve, 0)
            own[-1].start()
    for make, ways, ahead in ((z_hop, z_ways, Z_AHEAD), (y_hop, y_ways, len(y_ways[0]))):
        for way in ways:
            for up, s, p in way:
                if (up, s + 1, p) not in way:
                    make(up, s, p).wait_recv()
            for hop in way[-ahead:]:
                make(*hop).wait_send()
    for n in range(n_peers):
        ask(n).wait_send()
        near_give(n).wait()
    for k in range(1, n_mp):
        share(k).wait()
    for copy in own:
        copy.wait()


def spread(history, features, asks, weight, src_no, counts, n_mp):
    any_spec = pl.BlockSpec(memory_space=pl.ANY)
    smem_spec = pl.BlockSpec(memory_space=pltpu.SMEM)
    n_peers = NY * NC - 1

    def out(lead, value):
        return jax.ShapeDtypeStruct((lead,) + value.shape, value.dtype)

    cap = asks.shape[-1] // counts.shape[0]
    near = jax.ShapeDtypeStruct((NY * NC, cap) + history.shape[1:], history.dtype)

    return pl.pallas_call(
        spread_kernel,
        out_shape=(out(NZ, history), out(NY, features), out(NY * NC, asks), near, out(n_mp, weight),
                   jax.ShapeDtypeStruct(src_no.shape, jnp.int32)),
        in_specs=[any_spec] * 4 + [smem_spec] * 2,
        out_specs=(any_spec,) * 5 + (smem_spec,),
        scratch_shapes=[
            pltpu.VMEM(history.shape, history.dtype),
            pltpu.VMEM(features.shape, features.dtype),
            pltpu.VMEM(weight.shape, weight.dtype),
            pltpu.SMEM((NY * NC,) + asks.shape, asks.dtype),
            pltpu.VMEM(near.shape, near.dtype),
            pltpu.SemaphoreType.DMA((4,)),
            pltpu.SemaphoreType.DMA((5,)),
            pltpu.SemaphoreType.DMA((2, NZ // 2, Z_PIECES)),
            pltpu.SemaphoreType.DMA((2, NZ // 2, Z_PIECES)),
            pltpu.SemaphoreType.DMA((2, NY // 2, Y_PIECES)),
            pltpu.SemaphoreType.DMA((2, NY // 2, Y_PIECES)),
            pltpu.SemaphoreType.DMA((n_peers,)),
            pltpu.SemaphoreType.DMA((n_peers,)),
            pltpu.SemaphoreType.DMA((n_mp - 1,)),
            pltpu.SemaphoreType.DMA((n_mp - 1,)),
            pltpu.SemaphoreType.DMA((n_peers,)),
            pltpu.SemaphoreType.DMA((n_peers,)),
        ],
        compiler_params=pltpu.CompilerParams(
            collective_id=2, has_side_effects=True, vmem_limit_bytes=60 << 20
        ),
        name="spread",
    )(history, features, asks, weight, src_no, counts)


def pull_kernel(block_ids, hist, out, *scratch):
    shards = scratch[:NZ - 1]
    picked, load_sem, keep_sem, send_sems, recv_sems = scratch[NZ - 1:]
    y, z, core = lax.axis_index("y"), lax.axis_index("z"), lax.axis_index("core")
    cap = picked.shape[2]
    me = y * NC + core
    n_peers = NY * NC - 1
    per_ask = NY * NZ * NC * cap

    def peer(n):
        at = 3 * (n + 1) % (NC * NY)
        return (y + at // NC) % NY, (core + at % NC) % NC

    loads = [
        pltpu.make_async_copy(hist.at[(z + NZ - 1 - r) % NZ], shards[r], load_sem.at[r])
        for r in range(NZ - 1)
    ]
    for load in loads:
        load.start()
    barrier = pltpu.get_barrier_semaphore()
    for n in range(n_peers):
        to_y, to_core = peer(n)
        pl.semaphore_signal(
            barrier, inc=1, device_id={"y": to_y, "core": to_core}, device_id_type=MESH
        )
    pl.semaphore_wait(barrier, n_peers)

    def rows(r):
        return out.at[pl.ds((r * (n_peers + 1) + me) * cap, cap)]

    def give(r, n):
        to_y, to_core = peer(n)
        return pltpu.make_async_remote_copy(
            src_ref=picked.at[r, n],
            dst_ref=rows(r),
            send_sem=send_sems.at[r, n],
            recv_sem=recv_sems.at[r, n],
            device_id={"y": to_y, "core": to_core},
            device_id_type=MESH,
        )

    def keep(r):
        return pltpu.make_async_copy(picked.at[r, n_peers], rows(r), keep_sem.at[r])

    for r in range(NZ - 1):
        loads[r].wait()

        def one(n, carry):
            to_y, to_core = peer(n)
            first = (to_y * NC + to_core) * per_ask + ((y * NZ + (z + NZ - 1 - r) % NZ) * NC + core) * cap
            for slot in range(cap):
                picked[r, n, slot] = shards[r][block_ids[first + slot]]

            @pl.when(n < n_peers)
            def _():
                give(r, n).start()

            return carry

        lax.fori_loop(0, n_peers + 1, one, 0)
        keep(r).start()

    def finish(r, carry):
        def one(n, inner):
            give(r, n).wait()
            return inner

        lax.fori_loop(0, n_peers, one, 0)
        keep(r).wait()
        return carry

    lax.fori_loop(0, NZ - 1, finish, 0)


def pull(block_ids, hist):
    n_peers = NY * NC
    total = block_ids.shape[0] // n_peers
    cap = total // n_peers // NZ
    width = hist.shape[-1]
    any_spec = pl.BlockSpec(memory_space=pl.ANY)
    return pl.pallas_call(
        pull_kernel,
        out_shape=jax.ShapeDtypeStruct((total // NZ * (NZ - 1), BLK, width), jnp.bfloat16),
        in_specs=[pl.BlockSpec(memory_space=pltpu.SMEM), any_spec],
        out_specs=any_spec,
        scratch_shapes=[pltpu.VMEM(hist.shape[1:], jnp.bfloat16)] * (NZ - 1)
        + [
            pltpu.VMEM((NZ - 1, n_peers, cap, BLK, width), jnp.bfloat16),
            pltpu.SemaphoreType.DMA((NZ - 1,)),
            pltpu.SemaphoreType.DMA((NZ - 1,)),
            pltpu.SemaphoreType.DMA((NZ - 1, n_peers - 1)),
            pltpu.SemaphoreType.DMA((NZ - 1, n_peers - 1)),
        ],
        compiler_params=pltpu.CompilerParams(
            collective_id=1, has_side_effects=True, vmem_limit_bytes=60 << 20
        ),
        cost_estimate=pl.CostEstimate(flops=0, bytes_accessed=256 << 20, transcendentals=0),
        name="pull",
    )(block_ids, hist)


def per_device(
    features, history, adj_values, adj_sources, pull_list, pull_count, partner_mask, weight, bias
):
    row_count, width = features.shape
    row_blocks = row_count // BLK
    hist_blocks = history.shape[0] // BLK
    mask = partner_mask[0]
    n_mp = lax.axis_size("mp")
    y_mask = mask >> 4
    zc_mask = mask & (NZ * NC - 1)

    hist_z, feat_y, asked, near, wts, src_idx = spread(
        history.reshape(hist_blocks, BLK, width),
        features.reshape(Y_PIECES, row_count // Y_PIECES, width),
        pull_list.reshape(1, -1),
        weight,
        adj_sources.T,
        pull_count[0],
        n_mp,
    )

    half_way = lax.dynamic_index_in_dim(feat_y, lax.axis_index("y") ^ y_mask, keepdims=False)

    def pull_beside(m):
        def branch(rows, ids, hist):
            if m:
                rows = lax.ppermute(rows, ("z", "core"), [(s, s ^ m) for s in range(NZ * NC)])
            return rows, pull(ids, hist)

        return branch

    partner_rows, pulled = lax.switch(
        zc_mask,
        [pull_beside(m) for m in range(NZ * NC)],
        half_way,
        asked.reshape(-1),
        hist_z,
    )

    return layer(
        src_idx,
        features.reshape(row_blocks, BLK, width),
        partner_rows.reshape(row_blocks, BLK, width),
        near.reshape(-1, BLK, width),
        pulled,
        adj_values,
        half_way,
        wts,
        bias.reshape(1, width),
    )


def solution(mesh):
    n_mp = mesh.devices.shape[1]
    fine = Mesh(mesh.devices.reshape(NY, NZ, NC, n_mp), ("y", "z", "core", "mp"))
    in_specs = (
        P(DP, "mp"),
        P(DP, "mp"),
        P(DP, None, None, None),
        P(DP, None),
        P(DP, None, None),
        P(DP, None),
        P(),
        P("mp", None),
        P("mp"),
    )
    return jax.shard_map(
        per_device, mesh=fine, in_specs=in_specs, out_specs=P(DP, "mp"), check_vma=False
    )
```

```python
import jax
import jax.numpy as jnp
from jax import lax
from jax.experimental import pallas as pl
from jax.experimental.pallas import tpu as pltpu
from jax.sharding import Mesh, PartitionSpec as P

NY, NZ, NC = 4, 8, 2
BLK = 128
CHUNKS = 4
Z_PIECES = 4
Z_AHEAD = 2
Y_PIECES = 4
DP = ("y", "z", "core")
MESH = pl.DeviceIdType.MESH


def layer_kernel(
    n_mp, src_idx, own, partner, near, pulled, adj, unread, w_rows, my_bias,
    out, srcs, tiles, wts, bias, agg_out, agg_in, res_out,
    load_sem, w_sem, bias_send, bias_recv, send_a, recv_a, send_b, recv_b,
):
    me = lax.axis_index("mp")
    per_chunk, kb = adj.shape[2:4]
    nb, n_near, n_pulled = own.shape[0], near.shape[0], pulled.shape[0]
    n_src = 2 * nb + n_near + n_pulled
    rows = per_chunk * BLK

    def adj_load(q):
        return pltpu.make_async_copy(adj.at[:, q], tiles.at[:, q], load_sem.at[4 + q])

    loads = [
        pltpu.make_async_copy(own, srcs.at[pl.ds(0, nb)], load_sem.at[0]),
        pltpu.make_async_copy(partner, srcs.at[pl.ds(nb, nb)], load_sem.at[1]),
        pltpu.make_async_copy(near, srcs.at[pl.ds(2 * nb, n_near)], load_sem.at[2]),
        pltpu.make_async_copy(pulled, srcs.at[pl.ds(2 * nb + n_near, n_pulled)], load_sem.at[3]),
    ]
    for load in loads:
        load.start()
    adj_load(0).start()
    srcs[n_src] = jnp.zeros(srcs.shape[1:], srcs.dtype)

    barrier = pltpu.get_barrier_semaphore()
    for k in range(1, n_mp):
        pl.semaphore_signal(barrier, inc=1, device_id={"mp": (me + k) % n_mp}, device_id_type=MESH)
    pl.semaphore_wait(barrier, n_mp - 1)

    def to_bias(k):
        return pltpu.make_async_remote_copy(
            src_ref=my_bias,
            dst_ref=bias.at[k],
            send_sem=bias_send.at[k - 1],
            recv_sem=bias_recv.at[k - 1],
            device_id={"mp": (me + k) % n_mp},
            device_id_type=MESH,
        )

    for k in range(1, n_mp):
        to_bias(k).start()
    bias[0] = my_bias[...]
    for load in loads:
        load.wait()
    adj_load(0).wait()
    for q in range(1, CHUNKS):
        adj_load(q).start()
    cols = own.shape[-1]
    w_loads = [
        pltpu.make_async_copy(
            w_rows.at[k, :, pl.ds(n * cols, cols)], wts.at[k, n], w_sem.at[k, n]
        )
        for k in range(n_mp)
        for n in range(n_mp)
    ]
    for load in w_loads:
        load.start()
    for k in range(1, n_mp):
        to_bias(k).wait()

    def to_rows(q, k):
        return pltpu.make_async_remote_copy(
            src_ref=agg_out.at[q, k - 1],
            dst_ref=agg_in.at[q, k],
            send_sem=send_a.at[q, k - 1],
            recv_sem=recv_a.at[q, k - 1],
            device_id={"mp": (me + k) % n_mp},
            device_id_type=MESH,
        )

    def to_columns(q, k):
        return pltpu.make_async_remote_copy(
            src_ref=res_out.at[q, k - 1],
            dst_ref=out.at[pl.ds(pl.multiple_of((me * CHUNKS + q) * rows, rows), rows)],
            send_sem=send_b.at[q, k - 1],
            recv_sem=recv_b.at[q, k - 1],
            device_id={"mp": (me + k) % n_mp},
            device_id_type=MESH,
        )

    def aggregate(q, k, dst):
        dev = (me + k) % n_mp

        def one(i, carry):
            t = (dev * CHUNKS + q) * per_chunk + i
            lhs = jnp.concatenate([tiles[dev, q, i, j] for j in range(kb)], axis=1)
            rhs = jnp.concatenate([srcs[src_idx[j, t]] for j in range(kb)], axis=0)
            block = jnp.dot(lhs, rhs, preferred_element_type=jnp.float32)
            dst[pl.ds(pl.multiple_of(i * BLK, BLK), BLK), :] = block.astype(dst.dtype)
            return carry

        lax.fori_loop(0, per_chunk, one, 0, unroll=True)

    def multiply(q):
        for k in range(1, n_mp):
            to_rows(q, k).wait_recv()
        for n in list(range(1, n_mp)) + [0]:
            part = bias[(n_mp - n) % n_mp] + jnp.zeros((rows, 1), jnp.float32)
            for k in range(n_mp):
                part = part + jnp.dot(
                    agg_in[q, k], wts[k, (me + n) % n_mp], preferred_element_type=jnp.float32
                )
            part = jnp.maximum(part, 0.0).astype(out.dtype)
            if n:
                res_out[q, n - 1] = part
                to_columns(q, n).start()
            else:
                out[pl.ds(pl.multiple_of((me * CHUNKS + q) * rows, rows), rows), :] = part

    for q in range(CHUNKS + 1):
        if q < CHUNKS:
            if q:
                adj_load(q).wait()
            for k in (2, 1, 3):
                aggregate(q, k, agg_out.at[q, k - 1])
                to_rows(q, k).start()
            aggregate(q, 0, agg_in.at[q, 0])
        if q == 1:
            for load in w_loads:
                load.wait()
        if q:
            multiply(q - 1)
    for q in range(CHUNKS):
        for k in range(1, n_mp):
            to_rows(q, k).wait_send()
            to_columns(q, k).wait()


def layer(src_idx, own, partner, near, pulled, adj, unread, wts, bias):
    n_mp = wts.shape[0]
    tb, kb = adj.shape[:2]
    adj = adj.reshape(n_mp, CHUNKS, tb // n_mp // CHUNKS, kb, BLK, BLK)
    width = own.shape[-1]
    n_src = own.shape[0] + partner.shape[0] + near.shape[0] + pulled.shape[0]
    rows = tb // n_mp // CHUNKS * BLK
    any_spec = pl.BlockSpec(memory_space=pl.ANY)
    vmem_spec = pl.BlockSpec(memory_space=pltpu.VMEM)

    def kernel(*refs):
        layer_kernel(n_mp, *refs)

    return pl.pallas_call(
        kernel,
        out_shape=jax.ShapeDtypeStruct((tb * BLK, width), jnp.bfloat16),
        in_specs=[pl.BlockSpec(memory_space=pltpu.SMEM)] + [any_spec] * 7 + [vmem_spec],
        out_specs=vmem_spec,
        scratch_shapes=[
            pltpu.VMEM((n_src + 1, BLK, width), jnp.bfloat16),
            pltpu.VMEM(adj.shape, jnp.bfloat16),
            pltpu.VMEM((n_mp, n_mp, width, width), jnp.bfloat16),
            pltpu.VMEM((n_mp,) + bias.shape, jnp.float32),
            pltpu.VMEM((CHUNKS, n_mp - 1, rows, width), jnp.bfloat16),
            pltpu.VMEM((CHUNKS, n_mp, rows, width), jnp.bfloat16),
            pltpu.VMEM((CHUNKS, n_mp - 1, rows, width), jnp.bfloat16),
            pltpu.SemaphoreType.DMA((4 + CHUNKS,)),
            pltpu.SemaphoreType.DMA((n_mp, n_mp)),
            pltpu.SemaphoreType.DMA((n_mp - 1,)),
            pltpu.SemaphoreType.DMA((n_mp - 1,)),
        ]
        + [pltpu.SemaphoreType.DMA((CHUNKS, n_mp - 1))] * 4,
        compiler_params=pltpu.CompilerParams(
            collective_id=0, has_side_effects=True, vmem_limit_bytes=50 << 20
        ),
        name="layer",
    )(src_idx, own, partner, near, pulled, adj, unread, wts, bias)


def spread_kernel(
    hist, feat, asks, weight, src_no, counts, hist_z, feat_y, asked, near, wts, src_idx,
    hist_v, feat_v, weight_v, asked_s, picked, in_sem, own_sem,
    z_send, z_recv, y_send, y_recv, ask_send, ask_recv, w_send, w_recv, near_send, near_recv,
):
    y, z, core, mp = (lax.axis_index(name) for name in ("y", "z", "core", "mp"))
    n_mp = wts.shape[0]
    z_piece = hist.shape[0] // Z_PIECES
    n_targets = src_no.shape[1]
    own_blocks = feat.shape[0] * feat.shape[1] // BLK
    cap = asks.shape[-1] // counts.shape[0]
    n_peers = NY * NC - 1

    def peer(n):
        at = (n + 1) % (NY * NC)
        return (y + at // NC) % NY, (core + at % NC) % NC

    loads = [
        pltpu.make_async_copy(hist, hist_v, in_sem.at[0]),
        pltpu.make_async_copy(feat, feat_v, in_sem.at[1]),
        pltpu.make_async_copy(weight, weight_v, in_sem.at[2]),
    ]
    own = [
        pltpu.make_async_copy(hist_v, hist_z.at[z], own_sem.at[0]),
        pltpu.make_async_copy(feat_v, feat_y.at[y], own_sem.at[1]),
        pltpu.make_async_copy(weight_v, wts.at[0], own_sem.at[2]),
        pltpu.make_async_copy(picked.at[n_peers], near.at[y * NC + core], own_sem.at[4]),
    ]
    own_ask = pltpu.make_async_copy(asks, asked.at[y * NC + core], own_sem.at[3])
    for load in loads:
        load.start()

    barrier = pltpu.get_barrier_semaphore()
    for n in range(n_peers):
        to_y, to_core = peer(n)
        pl.semaphore_signal(
            barrier, inc=1, device_id={"y": to_y, "core": to_core}, device_id_type=MESH
        )
    for dz in (1, NZ - 1):
        pl.semaphore_signal(barrier, inc=1, device_id={"z": (z + dz) % NZ}, device_id_type=MESH)
    for k in range(1, n_mp):
        pl.semaphore_signal(barrier, inc=1, device_id={"mp": (mp + k) % n_mp}, device_id_type=MESH)
    pl.semaphore_wait(barrier, n_peers + 2 + n_mp - 1)

    def z_hop(up, s, p):
        at = (z + (1 - s if up else s - 1)) % NZ
        part = pl.ds(p * z_piece, z_piece)
        return pltpu.make_async_remote_copy(
            src_ref=(hist if s == 1 else hist_z.at[at]).at[part],
            dst_ref=hist_z.at[at, part],
            send_sem=z_send.at[0 if up else 1, s - 1, p],
            recv_sem=z_recv.at[0 if up else 1, s - 1, p],
            device_id={"z": (z + (1 if up else NZ - 1)) % NZ},
            device_id_type=MESH,
        )

    def y_hop(up, s, p):
        at = (y + (1 - s if up else s - 1)) % NY
        return pltpu.make_async_remote_copy(
            src_ref=(feat if s == 1 else feat_y.at[at]).at[p],
            dst_ref=feat_y.at[at, p],
            send_sem=y_send.at[0 if up else 1, s - 1, p],
            recv_sem=y_recv.at[0 if up else 1, s - 1, p],
            device_id={"y": (y + (1 if up else NY - 1)) % NY},
            device_id_type=MESH,
        )

    def order(size, pieces, up):
        last = range(pieces // 2) if up else range(pieces // 2, pieces)
        return [(up, s, p) for s in range(1, size // 2) for p in range(pieces)] + [
            (up, size // 2, p) for p in last
        ]

    def ask(n):
        to_y, to_core = peer(n)
        return pltpu.make_async_remote_copy(
            src_ref=asks,
            dst_ref=asked.at[y * NC + core],
            send_sem=ask_send.at[n],
            recv_sem=ask_recv.at[n],
            device_id={"y": to_y, "core": to_core},
            device_id_type=MESH,
        )

    def share(k):
        return pltpu.make_async_remote_copy(
            src_ref=weight,
            dst_ref=wts.at[k],
            send_sem=w_send.at[k - 1],
            recv_sem=w_recv.at[k - 1],
            device_id={"mp": (mp + k) % n_mp},
            device_id_type=MESH,
        )

    def place(t, carry):
        for j in range(src_no.shape[0]):
            src = src_no[j, t]
            at = jnp.maximum(src - 2 * own_blocks, 0)
            owner, slot = at // cap, at % cap
            oy, oz, oc = owner // (NZ * NC), owner // NC % NZ, owner % NC
            moved = (((z + NZ - oz) % NZ * NY + oy) * NC + oc) * cap + slot
            moved = jnp.where(slot < counts[owner], moved, counts.shape[0] * cap)
            src_idx[j, t] = jnp.where(src < 2 * own_blocks, src, 2 * own_blocks + moved)
        return carry

    z_ways = [order(NZ, Z_PIECES, up) for up in (True, False)]
    y_ways = [order(NY, Y_PIECES, up) for up in (True, False)]
    for n in range(n_peers):
        ask(n).start()
    own_ask.start()
    for way in z_ways:
        for hop in way[:Z_AHEAD]:
            z_hop(*hop).start()
    for load in loads:
        load.wait()

    own_ask.wait()
    for n in range(n_peers):
        ask(n).wait_recv()
    for way in y_ways:
        for hop in way[:Y_PIECES]:
            y_hop(*hop).start()
    for k in range(1, n_mp):
        share(k).start()
    index = pltpu.make_async_copy(asked, asked_s, in_sem.at[3])
    index.start()
    index.wait()

    def near_give(n):
        to_y, to_core = peer(n)
        return pltpu.make_async_remote_copy(
            src_ref=picked.at[n],
            dst_ref=near.at[y * NC + core],
            send_sem=near_send.at[n],
            recv_sem=near_recv.at[n],
            device_id={"y": to_y, "core": to_core},
            device_id_type=MESH,
        )

    def serve(n, carry):
        to_y, to_core = peer(n)
        for slot in range(cap):
            at = ((y * NZ + z) * NC + core) * cap + slot
            picked[n, slot] = hist_v[asked_s[to_y * NC + to_core, 0, at]]

        @pl.when(n < n_peers)
        def _():
            near_give(n).start()

        return carry

    lax.fori_loop(0, n_peers + 1, serve, 0)
    for copy in own:
        copy.start()

    for i in range(Z_AHEAD, len(z_ways[0])):
        for way in z_ways:
            up, s, p = way[i]
            z_hop(*way[i - Z_AHEAD]).wait_send()
            if s > 1:
                z_hop(up, s - 1, p).wait_recv()
            z_hop(up, s, p).start()
        some = -(-n_targets // (len(z_ways[0]) - Z_AHEAD))
        first = (i - Z_AHEAD) * some
        lax.fori_loop(first, min(first + some, n_targets), place, 0)
        if i == len(z_ways[0]) * 3 // 4:
            for way in y_ways:
                for up, s, p in way[Y_PIECES:]:
                    y_hop(up, s - 1, p).wait_recv()
                    y_hop(up, s, p).start()
    for make, ways, ahead in ((z_hop, z_ways, Z_AHEAD), (y_hop, y_ways, len(y_ways[0]))):
        for way in ways:
            for up, s, p in way:
                if (up, s + 1, p) not in way:
                    make(up, s, p).wait_recv()
            for hop in way[-ahead:]:
                make(*hop).wait_send()
    for n in range(n_peers):
        ask(n).wait_send()
        near_give(n).wait()
    for k in range(1, n_mp):
        share(k).wait()
    for copy in own:
        copy.wait()


def spread(history, features, asks, weight, src_no, counts, n_mp):
    any_spec = pl.BlockSpec(memory_space=pl.ANY)
    smem_spec = pl.BlockSpec(memory_space=pltpu.SMEM)
    n_peers = NY * NC - 1

    def out(lead, value):
        return jax.ShapeDtypeStruct((lead,) + value.shape, value.dtype)

    cap = asks.shape[-1] // counts.shape[0]
    near = jax.ShapeDtypeStruct((NY * NC, cap) + history.shape[1:], history.dtype)

    return pl.pallas_call(
        spread_kernel,
        out_shape=(out(NZ, history), out(NY, features), out(NY * NC, asks), near, out(n_mp, weight),
                   jax.ShapeDtypeStruct(src_no.shape, jnp.int32)),
        in_specs=[any_spec] * 4 + [smem_spec] * 2,
        out_specs=(any_spec,) * 5 + (smem_spec,),
        scratch_shapes=[
            pltpu.VMEM(history.shape, history.dtype),
            pltpu.VMEM(features.shape, features.dtype),
            pltpu.VMEM(weight.shape, weight.dtype),
            pltpu.SMEM((NY * NC,) + asks.shape, asks.dtype),
            pltpu.VMEM(near.shape, near.dtype),
            pltpu.SemaphoreType.DMA((4,)),
            pltpu.SemaphoreType.DMA((5,)),
            pltpu.SemaphoreType.DMA((2, NZ // 2, Z_PIECES)),
            pltpu.SemaphoreType.DMA((2, NZ // 2, Z_PIECES)),
            pltpu.SemaphoreType.DMA((2, NY // 2, Y_PIECES)),
            pltpu.SemaphoreType.DMA((2, NY // 2, Y_PIECES)),
            pltpu.SemaphoreType.DMA((n_peers,)),
            pltpu.SemaphoreType.DMA((n_peers,)),
            pltpu.SemaphoreType.DMA((n_mp - 1,)),
            pltpu.SemaphoreType.DMA((n_mp - 1,)),
            pltpu.SemaphoreType.DMA((n_peers,)),
            pltpu.SemaphoreType.DMA((n_peers,)),
        ],
        compiler_params=pltpu.CompilerParams(
            collective_id=2, has_side_effects=True, vmem_limit_bytes=60 << 20
        ),
        name="spread",
    )(history, features, asks, weight, src_no, counts)


def pull_kernel(block_ids, hist, out, *scratch):
    shards = scratch[:NZ - 1]
    picked, load_sem, keep_sem, send_sems, recv_sems = scratch[NZ - 1:]
    y, z, core = lax.axis_index("y"), lax.axis_index("z"), lax.axis_index("core")
    cap = picked.shape[2]
    me = y * NC + core
    n_peers = NY * NC - 1
    per_ask = NY * NZ * NC * cap

    def peer(n):
        at = 3 * (n + 1) % (NC * NY)
        return (y + at // NC) % NY, (core + at % NC) % NC

    loads = [
        pltpu.make_async_copy(hist.at[(z + NZ - 1 - r) % NZ], shards[r], load_sem.at[r])
        for r in range(NZ - 1)
    ]
    for load in loads:
        load.start()
    barrier = pltpu.get_barrier_semaphore()
    for n in range(n_peers):
        to_y, to_core = peer(n)
        pl.semaphore_signal(
            barrier, inc=1, device_id={"y": to_y, "core": to_core}, device_id_type=MESH
        )
    pl.semaphore_wait(barrier, n_peers)

    def rows(r):
        return out.at[pl.ds((r * (n_peers + 1) + me) * cap, cap)]

    def give(r, n):
        to_y, to_core = peer(n)
        return pltpu.make_async_remote_copy(
            src_ref=picked.at[r, n],
            dst_ref=rows(r),
            send_sem=send_sems.at[r, n],
            recv_sem=recv_sems.at[r, n],
            device_id={"y": to_y, "core": to_core},
            device_id_type=MESH,
        )

    def keep(r):
        return pltpu.make_async_copy(picked.at[r, n_peers], rows(r), keep_sem.at[r])

    for r in range(NZ - 1):
        loads[r].wait()

        def one(n, carry):
            to_y, to_core = peer(n)
            first = (to_y * NC + to_core) * per_ask + ((y * NZ + (z + NZ - 1 - r) % NZ) * NC + core) * cap
            for slot in range(cap):
                picked[r, n, slot] = shards[r][block_ids[first + slot]]

            @pl.when(n < n_peers)
            def _():
                give(r, n).start()

            return carry

        lax.fori_loop(0, n_peers + 1, one, 0)
        keep(r).start()

    def finish(r, carry):
        def one(n, inner):
            give(r, n).wait()
            return inner

        lax.fori_loop(0, n_peers, one, 0)
        keep(r).wait()
        return carry

    lax.fori_loop(0, NZ - 1, finish, 0)


def pull(block_ids, hist):
    n_peers = NY * NC
    total = block_ids.shape[0] // n_peers
    cap = total // n_peers // NZ
    width = hist.shape[-1]
    any_spec = pl.BlockSpec(memory_space=pl.ANY)
    return pl.pallas_call(
        pull_kernel,
        out_shape=jax.ShapeDtypeStruct((total // NZ * (NZ - 1), BLK, width), jnp.bfloat16),
        in_specs=[pl.BlockSpec(memory_space=pltpu.SMEM), any_spec],
        out_specs=any_spec,
        scratch_shapes=[pltpu.VMEM(hist.shape[1:], jnp.bfloat16)] * (NZ - 1)
        + [
            pltpu.VMEM((NZ - 1, n_peers, cap, BLK, width), jnp.bfloat16),
            pltpu.SemaphoreType.DMA((NZ - 1,)),
            pltpu.SemaphoreType.DMA((NZ - 1,)),
            pltpu.SemaphoreType.DMA((NZ - 1, n_peers - 1)),
            pltpu.SemaphoreType.DMA((NZ - 1, n_peers - 1)),
        ],
        compiler_params=pltpu.CompilerParams(
            collective_id=1, has_side_effects=True, vmem_limit_bytes=60 << 20
        ),
        cost_estimate=pl.CostEstimate(flops=0, bytes_accessed=256 << 20, transcendentals=0),
        name="pull",
    )(block_ids, hist)


def per_device(
    features, history, adj_values, adj_sources, pull_list, pull_count, partner_mask, weight, bias
):
    row_count, width = features.shape
    row_blocks = row_count // BLK
    hist_blocks = history.shape[0] // BLK
    mask = partner_mask[0]
    n_mp = lax.axis_size("mp")
    y_mask = mask >> 4
    zc_mask = mask & (NZ * NC - 1)

    hist_z, feat_y, asked, near, wts, src_idx = spread(
        history.reshape(hist_blocks, BLK, width),
        features.reshape(Y_PIECES, row_count // Y_PIECES, width),
        pull_list.reshape(1, -1),
        weight,
        adj_sources.T,
        pull_count[0],
        n_mp,
    )

    half_way = lax.dynamic_index_in_dim(feat_y, lax.axis_index("y") ^ y_mask, keepdims=False)

    def pull_beside(m):
        def branch(rows, ids, hist):
            if m:
                rows = lax.ppermute(rows, ("z", "core"), [(s, s ^ m) for s in range(NZ * NC)])
            return rows, pull(ids, hist)

        return branch

    partner_rows, pulled = lax.switch(
        zc_mask,
        [pull_beside(m) for m in range(NZ * NC)],
        half_way,
        asked.reshape(-1),
        hist_z,
    )

    return layer(
        src_idx,
        features.reshape(row_blocks, BLK, width),
        partner_rows.reshape(row_blocks, BLK, width),
        near.reshape(-1, BLK, width),
        pulled,
        adj_values,
        half_way,
        wts,
        bias.reshape(1, width),
    )


def solution(mesh):
    n_mp = mesh.devices.shape[1]
    fine = Mesh(mesh.devices.reshape(NY, NZ, NC, n_mp), ("y", "z", "core", "mp"))
    in_specs = (
        P(DP, "mp"),
        P(DP, "mp"),
        P(DP, None, None, None),
        P(DP, None),
        P(DP, None, None),
        P(DP, None),
        P(),
        P("mp", None),
        P("mp"),
    )
    return jax.shard_map(
        per_device, mesh=fine, in_specs=in_specs, out_specs=P(DP, "mp"), check_vma=False
    )
```
